512 devices in a mesh: side: 2 (over y_hi), grp: 8 (over z), dev: 32 (over x, y_lo, core).
Axes of the slice: x: 4, y: 8 (y_hi: 2, y_lo: 4; y = y_hi * 4 + y_lo), z: 8, core: 2. Of those that a mesh axis runs over, the one named last changes fastest.
Arguments:
- sources: float32 [2, 8, 65536], P('side', None, ('grp', 'dev')), may hold values from -2500 to 2500
- near_blocks: bfloat16 [2, 8192, 128, 128], P('side', ('grp', 'dev')), may hold values from -0.125 to 0.125
- block_rows: int32 [2, 8192], P('side', ('grp', 'dev')), may hold values from 0 to 1, as said below
- block_cols: int32 [2, 8192], P('side', ('grp', 'dev')), may hold values from 0 to 511, as said below
- mirror: int32 [65536], P(('grp', 'dev')), may hold values from 0 to 127, as said below
Outputs:
- krylov_basis: float32 [4, 2, 8, 65536], P(None, 'side', None, ('grp', 'dev'))
- hessenberg: float32 [8, 4, 3], replicated
The draws below stay inside these ranges and needn't reach their ends.
Inputs may be any that keep to these rules, and one draw needn't show every extreme that they name: `block_rows`: in each device's aligned run of 32 entries, the first 2 are 0 to 1 in order. `block_cols`: in each device's aligned run of 32 entries, the first 2 name that device's own blocks in order, and every entry names a block of an owner at most 4 owners before or after that device (owners of a half counted in the order grp, dev); where such owners exist, some entry names a block of the owner 4 before and some one of the owner 4 after. `mirror`: each aligned run of 128 entries is a permutation of 0 to 127.
All inputs are finite; a program needn't handle non-finite values.
Results may differ from the reference program's by a relative error of at most 0.005.
Values may be sent and summed in bfloat16 or wider, within the bound.
A program may use at most 64 MiB of HBM per device.

```python
import math
import jax
import jax.numpy as jnp
from jax import lax

BLOCK = 128
BLK_DEV = 2
NEAR = 16
WIN = 4
NRHS = 8
ITERS = 3
NB_DEV = 32
NBH = 512
NH = 65536
NBT = 8192
N_GRP = 8
N_DEV = 32


def draw_sources(key, part):
    keys = jax.random.split(jax.random.fold_in(key, 11), 3)
    shape = (2, NRHS, NH)
    position = (jnp.arange(2, dtype=jnp.float32)[:, None, None] * NH + jnp.arange(NH, dtype=jnp.float32)[None, None, :]) / (2.0 * NH)
    row_scale = jnp.exp(jax.random.uniform(keys[1], (2, 1, NH), jnp.float32, 0.0, math.log(10.0)))
    col_scale = jnp.exp(jax.random.uniform(keys[2], (1, NRHS, 1), jnp.float32, 0.0, math.log(10.0)))
    base = jnp.clip(jax.random.normal(keys[0], shape, jnp.float32), -4.0, 4.0)
    ramp = jnp.exp(math.log(3.0) * position)
    return base * row_scale * col_scale * ramp


def draw_block_rows(key, part):
    entry = jnp.arange(NBT, dtype=jnp.int32)
    within = entry % NB_DEV
    random_rows = jax.random.randint(jax.random.fold_in(key, 21), (2, NBT), 0, BLK_DEV, dtype=jnp.int32)
    return jnp.where(within[None, :] < BLK_DEV, within[None, :], random_rows).astype(jnp.int32)


def draw_block_cols(key, part):
    entry = jnp.arange(NBT, dtype=jnp.int32)
    within = entry % NB_DEV
    owner = entry // NB_DEV
    own_block = owner * BLK_DEV + within
    first_reach = (owner - WIN) * BLK_DEV
    last_reach = (owner + WIN + 1) * BLK_DEV - 1
    offsets = jax.random.randint(jax.random.fold_in(key, 31), (2, NBT), -WIN * BLK_DEV, (WIN + 1) * BLK_DEV, dtype=jnp.int32)
    random_cols = owner[None, :] * BLK_DEV + offsets
    chosen = jnp.where(within[None, :] == BLK_DEV, first_reach[None, :], random_cols)
    chosen = jnp.where(within[None, :] == BLK_DEV + 1, last_reach[None, :], chosen)
    chosen = jnp.clip(chosen, 0, NBH - 1)
    return jnp.where(within[None, :] < BLK_DEV, own_block[None, :], chosen).astype(jnp.int32)


def draw_mirror(key, part):
    keys = jax.random.split(jax.random.fold_in(key, 41), NBH)
    perms = jax.vmap(lambda single: jax.random.permutation(single, BLOCK))(keys)
    return perms.reshape(NH).astype(jnp.int32)


def levels(stream_key, extent, cuts, low, largest):
    gain, own = 1.0, jax.random.fold_in(stream_key, 6)
    for axis_at, shards_of in cuts:
        heights = jnp.exp(jax.random.uniform(jax.random.fold_in(own, axis_at), (shards_of,), jnp.float32, low / len(cuts), largest / len(cuts)))
        gain = gain * jnp.repeat(heights, extent[axis_at] // shards_of).reshape([-1 if axis == axis_at else 1 for axis in range(len(extent))])
    return gain


def gaussian(key, dims, scale, most, cuts=(), held_as=jnp.bfloat16):
    factor_of = levels(key, dims, cuts, -0.22, 0.18) if cuts else 1.0
    values = jax.random.normal(key, dims, jnp.float32) * scale * factor_of
    return jnp.minimum(jnp.maximum(values, -most), most).astype(held_as)


def setup_inputs(seed: int = 0) -> dict:
    seeds = jax.random.split(jax.random.key(seed), 6)
    sources = draw_sources(jax.random.fold_in(seeds[5], 71), 0)
    near_blocks = gaussian(seeds[1], (2, NBT, BLOCK, BLOCK), (NEAR * BLOCK) ** -0.5, 0.125, ((0, 2), (1, 256)))
    block_rows = draw_block_rows(jax.random.fold_in(seeds[5], 71), 0)
    block_cols = draw_block_cols(jax.random.fold_in(seeds[5], 71), 0)
    mirror = draw_mirror(jax.random.fold_in(seeds[5], 71), 0)
    return dict(sources=sources, near_blocks=near_blocks, block_rows=block_rows, block_cols=block_cols, mirror=mirror)


epsilon = 1e-06

def reference(sources, near_blocks, block_rows, block_cols, mirror):
    owners = N_GRP * N_DEV
    total_panels = 2.0 * NH
    vectors = sources.shape[1]
    mirror_onehot = (mirror.reshape(NBH, BLOCK)[:, :, None] == jnp.arange(BLOCK, dtype=jnp.int32)[None, None, :]).astype(jnp.float32)

    def mirrored(vector):
        shaped = vector.reshape(vectors, NBH, BLOCK)
        return jnp.einsum('bij,rbj->rbi', mirror_onehot, shaped, precision=lax.Precision.HIGHEST).reshape(vectors, NH)

    def unmirrored(vector):
        shaped = vector.reshape(vectors, NBH, BLOCK)
        return jnp.einsum('bij,rbi->rbj', mirror_onehot, shaped, precision=lax.Precision.HIGHEST).reshape(vectors, NH)

    def near_field(field, half):
        rounded = lax.optimization_barrier(field.astype(jnp.bfloat16)).astype(jnp.float32)
        field_blocks = rounded.reshape(vectors, NBH, BLOCK)
        all_blocks = near_blocks[half].reshape(owners, NB_DEV, BLOCK, BLOCK)
        all_rows = block_rows[half].reshape(owners, NB_DEV)
        all_cols = block_cols[half].reshape(owners, NB_DEV)

        def per_owner(pieces):
            owner_blocks, owner_rows, owner_cols = pieces
            picked = field_blocks[:, owner_cols]
            products = jnp.einsum('rkj,kij->rki', picked, owner_blocks.astype(jnp.float32), precision=lax.Precision.HIGHEST)
            row_onehot = (owner_rows[None, :] == jnp.arange(BLK_DEV, dtype=jnp.int32)[:, None]).astype(jnp.float32)
            return jnp.einsum('bk,rki->rbi', row_onehot, products, precision=lax.Precision.HIGHEST)
        summed = lax.map(per_owner, (all_blocks, all_rows, all_cols))
        summed = jnp.transpose(summed, (1, 0, 2, 3)).reshape(vectors, NH)
        return 0.5 * field + summed

    def operator(vector):
        symmetric = vector[0] + mirrored(vector[1])
        antisym = vector[0] - mirrored(vector[1])
        image_sym = near_field(symmetric, 0)
        image_anti = near_field(antisym, 1)
        return jnp.stack([0.5 * (image_sym + image_anti), unmirrored(0.5 * (image_sym - image_anti))])
    squares = lax.optimization_barrier(jnp.sum(sources * sources, axis=(0, 2))) / total_panels
    length = jnp.sqrt(squares + epsilon)
    vectors_list = [sources / length[None, :, None]]
    hessenberg = jnp.zeros((vectors, ITERS + 1, ITERS), jnp.float32)
    for column in range(ITERS):
        image = operator(vectors_list[column])
        stacked = jnp.stack(vectors_list)
        coeffs = lax.optimization_barrier(jnp.sum(image[None] * stacked, axis=(1, 3))) / total_panels
        remainder = image - jnp.einsum('jr,jsrp->srp', coeffs, stacked, precision=lax.Precision.HIGHEST)
        rem_norm = jnp.sqrt(lax.optimization_barrier(jnp.sum(remainder * remainder, axis=(0, 2))) / total_panels + epsilon)
        vectors_list.append(remainder / rem_norm[None, :, None])
        hessenberg = hessenberg.at[:, :column + 1, column].set(coeffs.T)
        hessenberg = hessenberg.at[:, column + 1, column].set(rem_norm)
    return (jnp.stack(vectors_list), hessenberg)
```

```python
import jax
import jax.numpy as jnp
from jax import lax
from jax.experimental import pallas as pl
from jax.experimental.pallas import tpu as pltpu
from jax.sharding import PartitionSpec as P

BLOCK = 128
BLK_DEV = 2
WIN = 4
ITERS = 3
NB_DEV = 32
NRHS = 8
N_GRP = 8
N_DEV = 32
TOTAL_PANELS = 131072.0
EPSILON = 1e-06
OWN = WIN * BLK_DEV
MESH = pl.DeviceIdType.MESH
PAIRS = [(i, j) for j in range(ITERS + 1) for i in range(j + 1)]


def lane_gather(x, index):
    return jnp.take_along_axis(x, index, axis=1, mode="promise_in_bounds")


def coefficients(gram):
    def dot(a, b):
        total = None
        for i, ai in enumerate(a):
            row = None
            for j, bj in enumerate(b):
                term = gram[(min(i, j), max(i, j))] * bj
                row = term if row is None else row + term
            total = ai * row if total is None else total + ai * row
        return total

    c = [[1.0 / jnp.sqrt(gram[(0, 0)] + EPSILON)]]
    h = {}
    for k in range(ITERS):
        w = [0.5 * v for v in c[k]] + [c[k][k]]
        for i in range(1, k + 1):
            w[i] = w[i] + c[k][i - 1]
        u = list(w)
        for j in range(k + 1):
            h[(j, k)] = dot(w, c[j])
            for i in range(j + 1):
                u[i] = u[i] - h[(j, k)] * c[j][i]
        norm = jnp.sqrt(jnp.maximum(dot(u, u), 0.0) + EPSILON)
        h[(k + 1, k)] = norm
        c.append([v / norm for v in u])
    return c, h


def kernel(
    x_ref, nb_hbm, rows_ref, cols_ref, mirror_ref, q_ref, h_ref,
    nb, win0, win1, win2, xs, xr, z3, zr, red,
    nb_sem, swap_send, swap_recv, halo_send, halo_recv, zx_send, zx_recv, red_send, red_recv,
):
    side = lax.axis_index("side")
    grp = lax.axis_index("grp")
    dev = lax.axis_index("dev")
    owner = grp * N_DEV + dev
    is_port = side == 0
    chip_x, y_lo, core = dev // 8, (dev // 2) % 4, dev % 2
    in_a = chip_x * 2 + core
    in_b = side * 4 + y_lo

    load = pltpu.make_async_copy(nb_hbm.at[0], nb, nb_sem)
    load.start()

    partner = (1 - side, grp, dev)

    def halo_device(distance):
        other = (owner + distance + N_GRP * N_DEV) % (N_GRP * N_DEV)
        return (side, other // N_DEV, other % N_DEV)

    def member(stage, flip):
        if stage == 0:
            other = in_a ^ flip
            return (side, grp, (other // 2) * 8 + y_lo * 2 + other % 2)
        if stage == 1:
            other = in_b ^ flip
            return (other // 4, grp, chip_x * 8 + (other % 4) * 2 + core)
        return (side, grp ^ flip, dev)

    slot = (in_a, in_b, grp)
    distances = [d for d in range(-WIN, WIN + 1) if d]

    barrier = pltpu.get_barrier_semaphore()
    met = [halo_device(d) for d in distances]
    met += [member(s, f) for s in range(3) for f in range(1, 8)]
    for device in met:
        pl.semaphore_signal(barrier, inc=1, device_id=device, device_id_type=MESH)

    index = [
        jnp.broadcast_to(mirror_ref[b : b + 1, :], (NRHS, BLOCK)) for b in range(BLK_DEV)
    ]
    own = [x_ref[0, :, b * BLOCK : (b + 1) * BLOCK] for b in range(BLK_DEV)]
    star = [lane_gather(own[b], index[b]) for b in range(BLK_DEV)]
    for b in range(BLK_DEV):
        xs[b] = jnp.where(is_port, own[b], star[b])

    pl.semaphore_wait(barrier, len(met))

    swap = pltpu.make_async_remote_copy(
        src_ref=xs, dst_ref=xr, send_sem=swap_send, recv_sem=swap_recv,
        device_id=partner, device_id_type=MESH,
    )
    swap.start()

    inverse = []
    for b in range(BLK_DEV):
        where_to = lax.broadcasted_iota(jnp.int32, (BLOCK, BLOCK), 0)
        onehot = jnp.where(
            jnp.broadcast_to(mirror_ref[b : b + 1, :], (BLOCK, BLOCK)) == where_to, 1.0, 0.0
        ).astype(jnp.bfloat16)
        lanes = lax.broadcasted_iota(jnp.int32, (16, BLOCK), 1).astype(jnp.float32).astype(jnp.bfloat16)
        found = lax.dot_general(
            lanes, onehot, (((1,), (1,)), ((), ())), preferred_element_type=jnp.float32
        )
        inverse.append(found[:NRHS].astype(jnp.int32))

    swap.wait_recv()
    z = [[None] * BLK_DEV for _ in range(ITERS + 1)]
    for b in range(BLK_DEV):
        other = xr[b]
        z[0][b] = jnp.where(is_port, own[b] + other, other - star[b])

    copies = [swap]
    exchanged = []
    load.wait()
    for k, win in enumerate((win0, win1, win2)):
        for b in range(BLK_DEV):
            win[OWN + b] = z[k][b].astype(jnp.bfloat16)
        hops = []
        for n, d in enumerate(distances):
            copy = pltpu.make_async_remote_copy(
                src_ref=win.at[pl.ds(OWN, BLK_DEV)],
                dst_ref=win.at[pl.ds((WIN - d) * BLK_DEV, BLK_DEV)],
                send_sem=halo_send.at[k, n],
                recv_sem=halo_recv.at[k, n],
                device_id=halo_device(d),
                device_id_type=MESH,
            )
            copy.start()
            hops.append(copy)
        copies += hops
        for copy in hops:
            copy.wait_recv()
        total = jnp.zeros((16, BLOCK), jnp.float32)
        for e in range(0, NB_DEV, 2):
            lefts, rights = [], []
            for f in (e, e + 1):
                place = cols_ref[0, f] - (owner - WIN) * BLK_DEV
                place = jnp.clip(place, 0, (2 * WIN + 1) * BLK_DEV - 1)
                picked = win[place].astype(jnp.float32)
                low = (rows_ref[0, f] == 0).astype(jnp.float32)
                lefts.append(
                    jnp.concatenate([picked * low, picked * (1.0 - low)], axis=0).astype(jnp.bfloat16)
                )
                rights.append(nb[f])
            total = total + lax.dot_general(
                jnp.concatenate(lefts, axis=1),
                jnp.concatenate(rights, axis=1),
                (((1,), (1,)), ((), ())),
                preferred_element_type=jnp.float32,
            )
        z[k + 1] = [total[:NRHS], total[NRHS:]]
        for b in range(BLK_DEV):
            z3[k, b] = z[k + 1][b]
        if k < ITERS:
            copy = pltpu.make_async_remote_copy(
                src_ref=z3.at[k], dst_ref=zr.at[k],
                send_sem=zx_send.at[k], recv_sem=zx_recv.at[k],
                device_id=partner, device_id_type=MESH,
            )
            copy.start()
            copies.append(copy)
            exchanged.append(copy)

    lane = lax.broadcasted_iota(jnp.int32, (NRHS, BLOCK), 1)
    partial = jnp.zeros((NRHS, BLOCK), jnp.float32)
    for p, (i, j) in enumerate(PAIRS):
        product = z[i][0] * z[j][0] + z[i][1] * z[j][1]
        partial = jnp.where(lane == p, jnp.sum(product, axis=1, keepdims=True), partial)

    for stage in range(3):
        red[stage, slot[stage]] = partial
        hops = []
        for flip in range(1, 8):
            copy = pltpu.make_async_remote_copy(
                src_ref=red.at[stage, slot[stage]],
                dst_ref=red.at[stage, slot[stage]],
                send_sem=red_send.at[stage, flip],
                recv_sem=red_recv.at[stage, flip],
                device_id=member(stage, flip),
                device_id_type=MESH,
            )
            copy.start()
            hops.append(copy)
        copies += hops
        if stage == 0:
            images = [own]
            for k in range(ITERS):
                exchanged[k].wait_recv()
                image = []
                for b in range(BLK_DEV):
                    mine, other = z[k + 1][b], zr[k, b]
                    port = 0.5 * (mine + other)
                    starboard = lane_gather(0.5 * (other - mine), inverse[b])
                    image.append(jnp.where(is_port, port, starboard))
                images.append(image)
        for copy in hops:
            copy.wait_recv()
        partial = red[stage, 0]
        for n in range(1, 8):
            partial = partial + red[stage, n]

    scaled = partial * (0.5 / TOTAL_PANELS)
    gram = {
        pair: jnp.broadcast_to(scaled[:, p : p + 1], (NRHS, BLOCK)) for p, pair in enumerate(PAIRS)
    }
    c, h = coefficients(gram)
    for j in range(ITERS + 1):
        for b in range(BLK_DEV):
            value = c[j][0] * images[0][b]
            for i in range(1, j + 1):
                value = value + c[j][i] * images[i][b]
            q_ref[j, 0, :, b * BLOCK : (b + 1) * BLOCK] = value
    table = jnp.zeros((NRHS, BLOCK), jnp.float32)
    for (j, k), value in h.items():
        table = jnp.where(lane == k * (ITERS + 1) + j, value, table)
    turned = jnp.transpose(table)
    for k in range(ITERS):
        h_ref[k] = turned[k * (ITERS + 1) : (k + 1) * (ITERS + 1), :]
    for copy in copies:
        copy.wait_send()


def on_device(sources, near_blocks, block_rows, block_cols, mirror):
    vmem = pl.BlockSpec(memory_space=pltpu.VMEM)
    smem = pl.BlockSpec(memory_space=pltpu.SMEM)
    f32, bf16 = jnp.float32, jnp.bfloat16
    dma = pltpu.SemaphoreType.DMA
    q, h = pl.pallas_call(
        kernel,
        out_shape=(
            jax.ShapeDtypeStruct((ITERS + 1, 1, NRHS, BLK_DEV * BLOCK), f32),
            jax.ShapeDtypeStruct((ITERS, ITERS + 1, NRHS), f32),
        ),
        in_specs=[vmem, pl.BlockSpec(memory_space=pl.ANY), smem, smem, vmem],
        out_specs=(vmem, vmem),
        scratch_shapes=[
            pltpu.VMEM((NB_DEV, BLOCK, BLOCK), bf16),
            *[pltpu.VMEM(((2 * WIN + 1) * BLK_DEV, NRHS, BLOCK), bf16)] * ITERS,
            pltpu.VMEM((BLK_DEV, NRHS, BLOCK), f32),
            pltpu.VMEM((BLK_DEV, NRHS, BLOCK), f32),
            pltpu.VMEM((ITERS, BLK_DEV, NRHS, BLOCK), f32),
            pltpu.VMEM((ITERS, BLK_DEV, NRHS, BLOCK), f32),
            pltpu.VMEM((3, 8, NRHS, BLOCK), f32),
            dma,
            dma, dma,
            dma((ITERS, 2 * WIN)), dma((ITERS, 2 * WIN)),
            dma((ITERS,)), dma((ITERS,)),
            dma((3, 8)), dma((3, 8)),
        ],
        compiler_params=pltpu.CompilerParams(
            collective_id=0, has_side_effects=True, vmem_limit_bytes=8 * 1024 * 1024
        ),
    )(sources, near_blocks, block_rows, block_cols, mirror.reshape(BLK_DEV, BLOCK))
    return q, jnp.transpose(h)


def solution(mesh):
    placed = (
        P("side", None, ("grp", "dev")),
        P("side", ("grp", "dev"), None, None),
        P("side", ("grp", "dev")),
        P("side", ("grp", "dev")),
        P(("grp", "dev")),
    )
    return jax.shard_map(
        on_device,
        mesh=mesh,
        in_specs=placed,
        out_specs=(P(None, "side", None, ("grp", "dev")), P()),
        check_vma=False,
    )
```

```python
import jax
import jax.numpy as jnp
from jax import lax
from jax.experimental import pallas as pl
from jax.experimental.pallas import tpu as pltpu
from jax.sharding import PartitionSpec as P

BLOCK = 128
BLK_DEV = 2
WIN = 4
ITERS = 3
NB_DEV = 32
NRHS = 8
N_GRP = 8
N_DEV = 32
TOTAL_PANELS = 131072.0
EPSILON = 1e-06
SLOTS = (2 * WIN + 1) * BLK_DEV
OWN = WIN * BLK_DEV
MESH = pl.DeviceIdType.MESH
PAIRS = [(i, j) for j in range(ITERS + 1) for i in range(j + 1)]
STAGE_SIZES = (16, 32)
DISTANCES = [4, -4, 3, -3, 2, -2, 1, -1]


def lane_gather(x, index):
    return jnp.take_along_axis(x, index, axis=1, mode="promise_in_bounds")


def coefficients(gram):
    def dot(a, b):
        total = None
        for i, ai in enumerate(a):
            row = None
            for j, bj in enumerate(b):
                term = gram[(min(i, j), max(i, j))] * bj
                row = term if row is None else row + term
            total = ai * row if total is None else total + ai * row
        return total

    c = [[1.0 / jnp.sqrt(gram[(0, 0)] + EPSILON)]]
    h = {}
    for k in range(ITERS):
        w = [0.5 * v for v in c[k]] + [c[k][k]]
        for i in range(1, k + 1):
            w[i] = w[i] + c[k][i - 1]
        u = list(w)
        for j in range(k + 1):
            h[(j, k)] = dot(w, c[j])
            for i in range(j + 1):
                u[i] = u[i] - h[(j, k)] * c[j][i]
        norm = jnp.sqrt(jnp.maximum(dot(u, u), 0.0) + EPSILON)
        h[(k + 1, k)] = norm
        c.append([v / norm for v in u])
    return c, h


def kernel(
    x_hbm, nb_hbm, rows_hbm, cols_hbm, mirror_hbm, q_ref, h_ref,
    x_ref, nb, rows_ref, cols_ref, mirror_ref,
    wina, winb, win1, win2, xs, xr, zs, zr, red0, red1,
    load_sem, swap_send, swap_recv, cross_send, cross_recv, halo_send, halo_recv,
    zx_send, zx_recv, red_send, red_recv,
):
    side = lax.axis_index("side")
    grp = lax.axis_index("grp")
    dev = lax.axis_index("dev")
    owner = grp * N_DEV + dev
    is_port = side == 0
    chip_x, y_lo, core = dev // 8, (dev // 2) % 4, dev % 2
    place = (grp * 2 + core, chip_x * 8 + side * 4 + y_lo)

    def near(distance, across):
        other = (owner + distance + N_GRP * N_DEV) % (N_GRP * N_DEV)
        return (1 - side if across else side, other // N_DEV, other % N_DEV)

    def member(stage, flip):
        other = place[stage] ^ flip
        if stage == 0:
            return (side, other // 2, chip_x * 8 + y_lo * 2 + other % 2)
        return ((other // 4) % 2, grp, (other // 8) * 8 + (other % 4) * 2 + core)

    barrier = pltpu.get_barrier_semaphore()
    met = [near(d, across) for d in DISTANCES for across in (False, True)]
    met += [member(s, f) for s in (1, 0) for f in range(1, STAGE_SIZES[s])]
    for device in met:
        pl.semaphore_signal(barrier, inc=1, device_id=device, device_id_type=MESH)

    loads = [
        pltpu.make_async_copy(source, target, load_sem.at[n])
        for n, (source, target) in enumerate(
            (
                (x_hbm, x_ref),
                (mirror_hbm, mirror_ref),
                (cols_hbm, cols_ref),
                (rows_hbm, rows_ref),
                (nb_hbm.at[0], nb),
            )
        )
    ]
    for load in loads:
        load.start()
    loads[0].wait()
    loads[1].wait()

    index = [
        jnp.broadcast_to(mirror_ref[b : b + 1, :], (NRHS, BLOCK)) for b in range(BLK_DEV)
    ]
    own = [x_ref[0, :, b * BLOCK : (b + 1) * BLOCK] for b in range(BLK_DEV)]
    star = [lane_gather(own[b], index[b]) for b in range(BLK_DEV)]
    for b in range(BLK_DEV):
        sent = jnp.where(is_port, own[b], star[b])
        xs[b] = sent
        wina[OWN + b] = sent.astype(jnp.bfloat16)

    pl.semaphore_wait(barrier, len(met))

    copies = []

    def send(source, target, send_sem, recv_sem, device):
        copy = pltpu.make_async_remote_copy(
            src_ref=source, dst_ref=target, send_sem=send_sem, recv_sem=recv_sem,
            device_id=device, device_id_type=MESH,
        )
        copy.start()
        copies.append(copy)
        return copy

    partner = (1 - side, grp, dev)
    swap = send(xs, xr, swap_send, swap_recv, partner)

    def halo(k, window, target, across, send_sem, recv_sem, n, d):
        return send(
            window.at[pl.ds(OWN, BLK_DEV)],
            target.at[pl.ds((WIN - d) * BLK_DEV, BLK_DEV)],
            send_sem, recv_sem, near(d, across),
        )

    hops = []
    for n, d in enumerate(DISTANCES):
        hops.append(halo(0, wina, wina, False, halo_send.at[0, n], halo_recv.at[0, n], n, d))
        hops.append(halo(0, wina, winb, True, cross_send.at[n], cross_recv.at[n], n, d))

    inverse = []
    for b in range(BLK_DEV):
        where_to = lax.broadcasted_iota(jnp.int32, (BLOCK, BLOCK), 0)
        onehot = jnp.where(
            jnp.broadcast_to(mirror_ref[b : b + 1, :], (BLOCK, BLOCK)) == where_to, 1.0, 0.0
        ).astype(jnp.bfloat16)
        lanes = lax.broadcasted_iota(jnp.int32, (16, BLOCK), 1).astype(jnp.float32).astype(jnp.bfloat16)
        found = lax.dot_general(
            lanes, onehot, (((1,), (1,)), ((), ())), preferred_element_type=jnp.float32
        )
        inverse.append(found[:NRHS].astype(jnp.int32))

    lane = lax.broadcasted_iota(jnp.int32, (NRHS, BLOCK), 1)
    sublane = lax.broadcasted_iota(jnp.int32, (NRHS, BLOCK), 0)
    sign = jnp.where(is_port, 1.0, -1.0)

    swap.wait_recv()
    z = [[None] * BLK_DEV for _ in range(ITERS + 1)]
    for b in range(BLK_DEV):
        z[0][b] = xr[b] + sign * xs[b]
        winb[OWN + b] = xr[b].astype(jnp.bfloat16)

    for load in loads[2:]:
        load.wait()
    where_from = [
        jnp.clip(cols_ref[0, e] - (owner - WIN) * BLK_DEV, 0, SLOTS - 1) for e in range(NB_DEV)
    ]
    upper = [(rows_ref[0, e] == 0).astype(jnp.float32) for e in range(NB_DEV)]

    def products(windows):
        total = jnp.zeros((16 * len(windows), BLOCK), jnp.float32)
        for e in range(0, NB_DEV, 2):
            lefts, rights = [], []
            for f in (e, e + 1):
                parts = []
                for window in windows:
                    picked = window[where_from[f]].astype(jnp.float32)
                    parts += [picked * upper[f], picked * (1.0 - upper[f])]
                lefts.append(jnp.concatenate(parts, axis=0).astype(jnp.bfloat16))
                rights.append(nb[f])
            total = total + lax.dot_general(
                jnp.concatenate(lefts, axis=1),
                jnp.concatenate(rights, axis=1),
                (((1,), (1,)), ((), ())),
                preferred_element_type=jnp.float32,
            )
        return total

    exchanged = []
    for k in range(ITERS):
        if k > 0:
            window = (None, win1, win2)[k]
            for b in range(BLK_DEV):
                window[OWN + b] = z[k][b].astype(jnp.bfloat16)
            hops = [
                halo(k, window, window, False, halo_send.at[k, n], halo_recv.at[k, n], n, d)
                for n, d in enumerate(DISTANCES)
            ]
            for b in range(BLK_DEV):
                zs[k - 1, b] = z[k][b]
            exchanged.append(
                send(zs.at[k - 1], zr.at[k - 1], zx_send.at[k - 1], zx_recv.at[k - 1], partner)
            )
        for copy in hops:
            copy.wait_recv()
        if k == 0:
            total = products([wina, winb])
            total = sign * total[:16] + total[16:]
        else:
            total = products([window])
        z[k + 1] = [total[:NRHS], total[NRHS:]]

    partial = jnp.zeros((NRHS, BLOCK), jnp.float32)
    for p, (i, j) in enumerate(PAIRS):
        product = z[i][0] * z[j][0] + z[i][1] * z[j][1]
        partial = jnp.where(
            lane == p * NRHS + sublane, jnp.sum(product, axis=1, keepdims=True), partial
        )
    row = jnp.sum(partial, axis=0, keepdims=True)

    for stage, red in enumerate((red0, red1)):
        size = STAGE_SIZES[stage]
        red[place[stage]] = row
        hops = [
            send(
                red.at[place[stage]], red.at[place[stage]],
                red_send.at[stage, flip], red_recv.at[stage, flip], member(stage, flip),
            )
            for flip in range(size - 1, 0, -1)
        ]
        if stage == 0:
            for b in range(BLK_DEV):
                zs[ITERS - 1, b] = z[ITERS][b]
            exchanged.append(
                send(
                    zs.at[ITERS - 1], zr.at[ITERS - 1],
                    zx_send.at[ITERS - 1], zx_recv.at[ITERS - 1], partner,
                )
            )
        if stage == 1:
            images = [own]
            for k in range(ITERS):
                exchanged[k].wait_recv()
                image = []
                for b in range(BLK_DEV):
                    mine, other = z[k + 1][b], zr[k, b]
                    port = 0.5 * (mine + other)
                    starboard = lane_gather(0.5 * (other - mine), inverse[b])
                    image.append(jnp.where(is_port, port, starboard))
                images.append(image)
        for copy in hops:
            copy.wait_recv()
        parts = [red[n] for n in range(size)]
        while len(parts) > 1:
            parts = [a + b for a, b in zip(parts[::2], parts[1::2], strict=True)]
        row = parts[0]

    spread = jnp.broadcast_to(row * (0.5 / TOTAL_PANELS), (NRHS, BLOCK))
    gram = {}
    for p, pair in enumerate(PAIRS):
        chosen = jnp.where(lane == p * NRHS + sublane, spread, 0.0)
        gram[pair] = jnp.broadcast_to(jnp.sum(chosen, axis=1, keepdims=True), (NRHS, BLOCK))
    c, h = coefficients(gram)
    for j in range(ITERS + 1):
        for b in range(BLK_DEV):
            value = c[j][0] * images[0][b]
            for i in range(1, j + 1):
                value = value + c[j][i] * images[i][b]
            q_ref[j, 0, :, b * BLOCK : (b + 1) * BLOCK] = value
    table = jnp.zeros((NRHS, BLOCK), jnp.float32)
    for (j, k), value in h.items():
        table = jnp.where(lane == k * (ITERS + 1) + j, value, table)
    turned = jnp.transpose(table)
    for k in range(ITERS):
        h_ref[k] = turned[k * (ITERS + 1) : (k + 1) * (ITERS + 1), :]
    for copy in copies:
        copy.wait_send()


def on_device(sources, near_blocks, block_rows, block_cols, mirror):
    vmem = pl.BlockSpec(memory_space=pltpu.VMEM)
    hbm = pl.BlockSpec(memory_space=pltpu.HBM)
    f32, bf16 = jnp.float32, jnp.bfloat16
    dma = pltpu.SemaphoreType.DMA
    window = pltpu.VMEM((SLOTS, NRHS, BLOCK), bf16)
    blocks = pltpu.VMEM((BLK_DEV, NRHS, BLOCK), f32)
    steps = pltpu.VMEM((ITERS, BLK_DEV, NRHS, BLOCK), f32)
    q, h = pl.pallas_call(
        kernel,
        out_shape=(
            jax.ShapeDtypeStruct((ITERS + 1, 1, NRHS, BLK_DEV * BLOCK), f32),
            jax.ShapeDtypeStruct((ITERS, ITERS + 1, NRHS), f32),
        ),
        in_specs=[hbm] * 5,
        out_specs=(vmem, vmem),
        scratch_shapes=[
            pltpu.VMEM((1, NRHS, BLK_DEV * BLOCK), f32),
            pltpu.VMEM((NB_DEV, BLOCK, BLOCK), bf16),
            pltpu.SMEM((1, NB_DEV), jnp.int32),
            pltpu.SMEM((1, NB_DEV), jnp.int32),
            pltpu.VMEM((BLK_DEV, BLOCK), jnp.int32),
            window, window, window, window,
            blocks, blocks,
            steps, steps,
            *[pltpu.VMEM((size, 1, BLOCK), f32) for size in STAGE_SIZES],
            dma((5,)),
            dma, dma,
            dma((2 * WIN,)), dma((2 * WIN,)),
            dma((ITERS, 2 * WIN)), dma((ITERS, 2 * WIN)),
            dma((ITERS,)), dma((ITERS,)),
            dma((2, 32)), dma((2, 32)),
        ],
        compiler_params=pltpu.CompilerParams(
            collective_id=0, has_side_effects=True, vmem_limit_bytes=8 * 1024 * 1024
        ),
    )(
        *[
            pltpu.with_memory_space_constraint(operand, pltpu.HBM)
            for operand in (
                sources, near_blocks, block_rows, block_cols, mirror.reshape(BLK_DEV, BLOCK)
            )
        ]
    )
    return q, jnp.transpose(h)


def solution(mesh):
    placed = (
        P("side", None, ("grp", "dev")),
        P("side", ("grp", "dev"), None, None),
        P("side", ("grp", "dev")),
        P("side", ("grp", "dev")),
        P(("grp", "dev")),
    )
    return jax.shard_map(
        on_device,
        mesh=mesh,
        in_specs=placed,
        out_specs=(P(None, "side", None, ("grp", "dev")), P()),
        check_vma=False,
    )
```

```python
import jax
import jax.numpy as jnp
from jax import lax
from jax.experimental import pallas as pl
from jax.experimental.pallas import tpu as pltpu
from jax.sharding import PartitionSpec as P

BLOCK = 128
BLK_DEV = 2
WIN = 4
ITERS = 3
NB_DEV = 32
NRHS = 8
N_GRP = 8
N_DEV = 32
TOTAL_PANELS = 131072.0
EPSILON = 1e-06
SLOTS = (2 * WIN + 1) * BLK_DEV
OWN = WIN * BLK_DEV
MESH = pl.DeviceIdType.MESH
PAIRS = [(i, j) for j in range(ITERS + 1) for i in range(j + 1)]
N_OWNERS = N_GRP * N_DEV
STAGE_SIZES = (16, 32)
EARLY = N_GRP // 2
X_HOPS = (0, 1, 2, 1)
Y_HOPS = (0, 1, 2, 3, 4, 3, 2, 3)
FLIPS = sorted(range(1, 32), key=lambda f: -X_HOPS[f // 8] - Y_HOPS[f % 8])
DISTANCES = [4, -4, 3, -3, 2, -2, 1, -1]


def lane_gather(x, index):
    return jnp.take_along_axis(x, index, axis=1, mode="promise_in_bounds")


def coefficients(gram):
    def dot(a, b):
        total = None
        for i, ai in enumerate(a):
            row = None
            for j, bj in enumerate(b):
                term = gram[(min(i, j), max(i, j))] * bj
                row = term if row is None else row + term
            total = ai * row if total is None else total + ai * row
        return total

    c = [[1.0 / jnp.sqrt(gram[(0, 0)] + EPSILON)]]
    h = {}
    for k in range(ITERS):
        w = [0.5 * v for v in c[k]] + [c[k][k]]
        for i in range(1, k + 1):
            w[i] = w[i] + c[k][i - 1]
        u = list(w)
        for j in range(k + 1):
            h[(j, k)] = dot(w, c[j])
            for i in range(j + 1):
                u[i] = u[i] - h[(j, k)] * c[j][i]
        norm = jnp.sqrt(jnp.maximum(dot(u, u), 0.0) + EPSILON)
        h[(k + 1, k)] = norm
        c.append([v / norm for v in u])
    return c, h


def kernel(
    x_hbm, nb_hbm, rows_hbm, cols_hbm, mirror_hbm, q_ref, h_ref,
    x_ref, nb, rows_ref, cols_ref, mirror_ref,
    wina, winb, win1, win2, xs, xr, zs, zr, red0, red1, total_ref,
    load_sem, swap_send, swap_recv, middle_send, middle_recv, cross_send, cross_recv, halo_send, halo_recv,
    zx_send, zx_recv, red_send, red_recv, pass_send, pass_recv,
):
    side = lax.axis_index("side")
    grp = lax.axis_index("grp")
    dev = lax.axis_index("dev")
    owner = grp * N_DEV + dev
    is_port = side == 0
    chip_x, y_lo, core = dev // 8, (dev // 2) % 4, dev % 2
    is_early = grp < EARLY
    is_edge = (owner < WIN) | (owner >= N_OWNERS - WIN)
    column = grp * 2 + core
    spot = chip_x * 8 + side * 4 + y_lo

    def exists(distance):
        return (owner + distance >= 0) & (owner + distance < N_OWNERS)

    def near(distance, across):
        other = owner + distance
        return (1 - side if across else side, other // N_DEV, other % N_DEV)

    def in_column(flip, half):
        return (side, half + (grp % EARLY ^ (flip // 2)), chip_x * 8 + y_lo * 2 + (core ^ (flip % 2)))

    def in_plane(flip):
        other = spot ^ flip
        return ((other // 4) % 2, grp, (other // 8) * 8 + (other % 4) * 2 + core)

    def for_each(items, act, forward=True):
        @pl.when(jnp.logical_not(is_edge))
        def _():
            for _, item in items:
                act(item)

        @pl.when(is_edge)
        def _():
            for d, item in items:

                @pl.when(exists(d if forward else -d))
                def _(item=item):
                    act(item)

    barrier = pltpu.get_barrier_semaphore()

    def greet(device):
        pl.semaphore_signal(barrier, inc=1, device_id=device, device_id_type=MESH)

    neighbours = [(d, near(d, across)) for d in DISTANCES for across in (False, True)]
    partner = (1 - side, grp, dev)
    greet(partner)
    for_each(neighbours, greet)

    @pl.when(is_early)
    def _():
        for flip in FLIPS:
            greet(in_plane(flip))
        for flip in range(1, 8):
            greet(in_column(flip, 0))
        for flip in range(8):
            greet(in_column(flip, EARLY))

    loads = [
        pltpu.make_async_copy(source, target, load_sem.at[n])
        for n, (source, target) in enumerate(
            (
                (x_hbm, x_ref),
                (mirror_hbm, mirror_ref),
                (cols_hbm, cols_ref),
                (rows_hbm, rows_ref),
                (nb_hbm.at[0], nb),
            )
        )
    ]
    for load in loads:
        load.start()
    loads[0].wait()
    loads[1].wait()

    index = [
        jnp.broadcast_to(mirror_ref[b : b + 1, :], (NRHS, BLOCK)) for b in range(BLK_DEV)
    ]
    own = [x_ref[0, :, b * BLOCK : (b + 1) * BLOCK] for b in range(BLK_DEV)]
    star = [lane_gather(own[b], index[b]) for b in range(BLK_DEV)]
    for b in range(BLK_DEV):
        sent = jnp.where(is_port, own[b], star[b])
        xs[b] = sent
        wina[OWN + b] = sent.astype(jnp.bfloat16)

    present = 1
    for d in DISTANCES:
        present = present + 2 * exists(d).astype(jnp.int32)
    pl.semaphore_wait(barrier, present + jnp.where(is_early, len(FLIPS) + 7, 8))

    def remote(source, target, send_sem, recv_sem, device):
        return pltpu.make_async_remote_copy(
            src_ref=source, dst_ref=target, send_sem=send_sem, recv_sem=recv_sem,
            device_id=device, device_id_type=MESH,
        )

    def start(copy):
        copy.start()

    def received(copy):
        copy.wait_recv()

    def sent_off(copy):
        copy.wait_send()

    swap = remote(xs, xr, swap_send, swap_recv, partner)
    copies, hop_copies = [swap], []

    def halo(window, target, across, send_sem, recv_sem):
        return [
            (
                d,
                remote(
                    window.at[pl.ds(OWN, BLK_DEV)],
                    target.at[pl.ds((WIN - d) * BLK_DEV, BLK_DEV)],
                    send_sem.at[n], recv_sem.at[n], near(d, across),
                ),
            )
            for n, d in enumerate(DISTANCES)
        ]

    middle = remote(
        wina.at[pl.ds(OWN, BLK_DEV)], winb.at[pl.ds(OWN, BLK_DEV)], middle_send, middle_recv, partner
    )
    start(middle)
    copies.append(middle)
    hops = halo(wina, winb, True, cross_send, cross_recv)
    hops += halo(wina, wina, False, halo_send.at[0], halo_recv.at[0])
    for_each(hops, start)
    start(swap)
    hop_copies += hops

    inverse = []
    for b in range(BLK_DEV):
        where_to = lax.broadcasted_iota(jnp.int32, (BLOCK, BLOCK), 0)
        onehot = jnp.where(
            jnp.broadcast_to(mirror_ref[b : b + 1, :], (BLOCK, BLOCK)) == where_to, 1.0, 0.0
        ).astype(jnp.bfloat16)
        lanes = lax.broadcasted_iota(jnp.int32, (16, BLOCK), 1).astype(jnp.float32).astype(jnp.bfloat16)
        found = lax.dot_general(
            lanes, onehot, (((1,), (1,)), ((), ())), preferred_element_type=jnp.float32
        )
        inverse.append(found[:NRHS].astype(jnp.int32))

    lane = lax.broadcasted_iota(jnp.int32, (NRHS, BLOCK), 1)
    sublane = lax.broadcasted_iota(jnp.int32, (NRHS, BLOCK), 0)
    sign = jnp.where(is_port, 1.0, -1.0)

    z = [[None] * BLK_DEV for _ in range(ITERS + 1)]
    for load in loads[2:]:
        load.wait()
    where_from = [
        jnp.clip(cols_ref[0, e] - (owner - WIN) * BLK_DEV, 0, SLOTS - 1) for e in range(NB_DEV)
    ]
    upper = [(rows_ref[0, e] == 0).astype(jnp.float32) for e in range(NB_DEV)]

    def products(windows):
        total = jnp.zeros((16 * len(windows), BLOCK), jnp.float32)
        for e in range(0, NB_DEV, 2):
            lefts, rights = [], []
            for f in (e, e + 1):
                parts = []
                for window in windows:
                    picked = window[where_from[f]].astype(jnp.float32)
                    parts += [picked * upper[f], picked * (1.0 - upper[f])]
                lefts.append(jnp.concatenate(parts, axis=0).astype(jnp.bfloat16))
                rights.append(nb[f])
            total = total + lax.dot_general(
                jnp.concatenate(lefts, axis=1),
                jnp.concatenate(rights, axis=1),
                (((1,), (1,)), ((), ())),
                preferred_element_type=jnp.float32,
            )
        return total

    exchanged = []
    for k in range(ITERS):
        if k > 0:
            window = (None, win1, win2)[k]
            for b in range(BLK_DEV):
                window[OWN + b] = z[k][b].astype(jnp.bfloat16)
            hops = halo(window, window, False, halo_send.at[k], halo_recv.at[k])
            for_each(hops, start)
            hop_copies += hops
            for b in range(BLK_DEV):
                zs[k - 1, b] = z[k][b]
            exchanged.append(
                remote(zs.at[k - 1], zr.at[k - 1], zx_send.at[k - 1], zx_recv.at[k - 1], partner)
            )
            start(exchanged[-1])
        for_each(hops, received, forward=False)
        if k == 0:
            received(middle)
            total = products([wina, winb])
            total = sign * total[:16] + total[16:]
        else:
            total = products([window])
        z[k + 1] = [total[:NRHS], total[NRHS:]]

    received(swap)
    for b in range(BLK_DEV):
        z[0][b] = xr[b] + sign * xs[b]
    partial = jnp.zeros((NRHS, BLOCK), jnp.float32)
    for p, (i, j) in enumerate(PAIRS):
        product = z[i][0] * z[j][0] + z[i][1] * z[j][1]
        partial = jnp.where(
            lane == p * NRHS + sublane, jnp.sum(product, axis=1, keepdims=True), partial
        )
    row = jnp.sum(partial, axis=0, keepdims=True)

    def total_of(red, size):
        parts = [red[n] for n in range(size)]
        while len(parts) > 1:
            parts = [a + b for a, b in zip(parts[::2], parts[1::2], strict=True)]
        return parts[0]

    red0[column] = row

    def to_column(flip, is_late):
        kind = 8 * is_late + flip
        return remote(
            red0.at[column], red0.at[column], red_send.at[flip], red_recv.at[0, kind], in_column(flip, 0)
        )

    early_copies = [to_column(flip, 0) for flip in range(8)]
    late_copies = [to_column(flip, 1) for flip in range(8)]

    @pl.when(is_early)
    def _():
        for copy in early_copies[1:]:
            start(copy)

    @pl.when(jnp.logical_not(is_early))
    def _():
        for copy in late_copies:
            start(copy)

    for b in range(BLK_DEV):
        zs[ITERS - 1, b] = z[ITERS][b]
    exchanged.append(
        remote(
            zs.at[ITERS - 1], zr.at[ITERS - 1], zx_send.at[ITERS - 1], zx_recv.at[ITERS - 1], partner
        )
    )
    start(exchanged[-1])
    copies += exchanged

    plane_copies = [
        remote(red1.at[spot], red1.at[spot], red_send.at[flip], red_recv.at[1, flip], in_plane(flip))
        for flip in FLIPS
    ]
    pass_on = remote(
        total_ref, total_ref, pass_send, pass_recv, (side, grp % EARLY + EARLY, dev)
    )

    @pl.when(is_early)
    def _():
        for copy in early_copies[1:] + late_copies:
            received(copy)
        for copy in early_copies[1:]:
            sent_off(copy)
        red1[spot] = total_of(red0, STAGE_SIZES[0])
        for copy in plane_copies:
            start(copy)

    images = [own]
    for k in range(ITERS):
        received(exchanged[k])
        image = []
        for b in range(BLK_DEV):
            mine, other = z[k + 1][b], zr[k, b]
            port = 0.5 * (mine + other)
            starboard = lane_gather(0.5 * (other - mine), inverse[b])
            image.append(jnp.where(is_port, port, starboard))
        images.append(image)

    @pl.when(is_early)
    def _():
        for copy in plane_copies:
            received(copy)
        total_ref[...] = total_of(red1, STAGE_SIZES[1])
        start(pass_on)

    @pl.when(jnp.logical_not(is_early))
    def _():
        received(pass_on)

    row = total_ref[...]
    spread = jnp.broadcast_to(row * (0.5 / TOTAL_PANELS), (NRHS, BLOCK))
    gram = {}
    for p, pair in enumerate(PAIRS):
        chosen = jnp.where(lane == p * NRHS + sublane, spread, 0.0)
        gram[pair] = jnp.broadcast_to(jnp.sum(chosen, axis=1, keepdims=True), (NRHS, BLOCK))
    c, h = coefficients(gram)
    for j in range(ITERS + 1):
        for b in range(BLK_DEV):
            value = c[j][0] * images[0][b]
            for i in range(1, j + 1):
                value = value + c[j][i] * images[i][b]
            q_ref[j, 0, :, b * BLOCK : (b + 1) * BLOCK] = value
    table = jnp.zeros((NRHS, BLOCK), jnp.float32)
    for (j, k), value in h.items():
        table = jnp.where(lane == k * (ITERS + 1) + j, value, table)
    turned = jnp.transpose(table)
    for k in range(ITERS):
        h_ref[k] = turned[k * (ITERS + 1) : (k + 1) * (ITERS + 1), :]
    for copy in copies:
        sent_off(copy)
    for_each(hop_copies, sent_off)

    @pl.when(is_early)
    def _():
        for copy in plane_copies:
            sent_off(copy)
        sent_off(pass_on)

    @pl.when(jnp.logical_not(is_early))
    def _():
        for copy in late_copies:
            sent_off(copy)


def settle(q_ref, h_ref, q_out, h_out, sem):
    moves = [
        pltpu.make_async_copy(q_ref, q_out, sem.at[0]),
        pltpu.make_async_copy(h_ref, h_out, sem.at[1]),
    ]
    for move in moves:
        move.start()
    for move in moves:
        move.wait()


def on_device(sources, near_blocks, block_rows, block_cols, mirror):
    vmem = pl.BlockSpec(memory_space=pltpu.VMEM)
    hbm = pl.BlockSpec(memory_space=pltpu.HBM)
    f32, bf16 = jnp.float32, jnp.bfloat16
    dma = pltpu.SemaphoreType.DMA
    window = pltpu.VMEM((SLOTS, NRHS, BLOCK), bf16)
    blocks = pltpu.VMEM((BLK_DEV, NRHS, BLOCK), f32)
    steps = pltpu.VMEM((ITERS, BLK_DEV, NRHS, BLOCK), f32)
    q, h = pl.pallas_call(
        kernel,
        out_shape=(
            jax.ShapeDtypeStruct((ITERS + 1, 1, NRHS, BLK_DEV * BLOCK), f32),
            jax.ShapeDtypeStruct((ITERS, ITERS + 1, NRHS), f32),
        ),
        in_specs=[hbm] * 5,
        out_specs=(vmem, vmem),
        scratch_shapes=[
            pltpu.VMEM((1, NRHS, BLK_DEV * BLOCK), f32),
            pltpu.VMEM((NB_DEV, BLOCK, BLOCK), bf16),
            pltpu.SMEM((1, NB_DEV), jnp.int32),
            pltpu.SMEM((1, NB_DEV), jnp.int32),
            pltpu.VMEM((BLK_DEV, BLOCK), jnp.int32),
            window, window, window, window,
            blocks, blocks,
            steps, steps,
            *[pltpu.VMEM((size, 1, BLOCK), f32) for size in STAGE_SIZES],
            pltpu.VMEM((1, BLOCK), f32),
            dma((5,)),
            dma, dma,
            dma, dma,
            dma((2 * WIN,)), dma((2 * WIN,)),
            dma((ITERS, 2 * WIN)), dma((ITERS, 2 * WIN)),
            dma((ITERS,)), dma((ITERS,)),
            dma((32,)), dma((2, 32)),
            dma, dma,
        ],
        compiler_params=pltpu.CompilerParams(
            collective_id=0, has_side_effects=True, vmem_limit_bytes=8 * 1024 * 1024
        ),
    )(
        *[
            pltpu.with_memory_space_constraint(operand, pltpu.HBM)
            for operand in (
                sources, near_blocks, block_rows, block_cols, mirror.reshape(BLK_DEV, BLOCK)
            )
        ]
    )
    q, h = pl.pallas_call(
        settle,
        out_shape=(
            jax.ShapeDtypeStruct(q.shape, f32),
            jax.ShapeDtypeStruct(h.shape, f32),
        ),
        in_specs=[vmem, vmem],
        out_specs=(hbm, hbm),
        scratch_shapes=[dma((2,))],
        compiler_params=pltpu.CompilerParams(vmem_limit_bytes=8 * 1024 * 1024),
    )(q, h)
    return q, jnp.transpose(h)


def solution(mesh):
    placed = (
        P("side", None, ("grp", "dev")),
        P("side", ("grp", "dev"), None, None),
        P("side", ("grp", "dev")),
        P("side", ("grp", "dev")),
        P(("grp", "dev")),
    )
    return jax.shard_map(
        on_device,
        mesh=mesh,
        in_specs=placed,
        out_specs=(P(None, "side", None, ("grp", "dev")), P()),
        check_vma=False,
    )
```

```python
import jax
import jax.numpy as jnp
from jax import lax
from jax.experimental import pallas as pl
from jax.experimental.pallas import tpu as pltpu
from jax.sharding import PartitionSpec as P

BLOCK = 128
BLK_DEV = 2
WIN = 4
ITERS = 3
NB_DEV = 32
NRHS = 8
N_GRP = 8
N_DEV = 32
TOTAL_PANELS = 131072.0
EPSILON = 1e-06
SLOTS = (2 * WIN + 1) * BLK_DEV
OWN = WIN * BLK_DEV
MESH = pl.DeviceIdType.MESH
PAIRS = [(i, j) for j in range(ITERS + 1) for i in range(j + 1)]
N_OWNERS = N_GRP * N_DEV
STAGE_SIZES = (16, 32)
EARLY = N_GRP // 2
X_HOPS = (0, 1, 2, 1)
Y_HOPS = (0, 1, 2, 3, 4, 3, 2, 3)
FLIPS = sorted(range(1, 32), key=lambda f: -X_HOPS[f // 8] - Y_HOPS[f % 8])
DISTANCES = [4, -4, 3, -3, 2, -2, 1, -1]


def lane_gather(x, index):
    return jnp.take_along_axis(x, index, axis=1, mode="promise_in_bounds")


def coefficients(gram):
    def dot(a, b):
        total = None
        for i, ai in enumerate(a):
            row = None
            for j, bj in enumerate(b):
                term = gram[(min(i, j), max(i, j))] * bj
                row = term if row is None else row + term
            total = ai * row if total is None else total + ai * row
        return total

    c = [[1.0 / jnp.sqrt(gram[(0, 0)] + EPSILON)]]
    h = {}
    for k in range(ITERS):
        w = [0.5 * v for v in c[k]] + [c[k][k]]
        for i in range(1, k + 1):
            w[i] = w[i] + c[k][i - 1]
        u = list(w)
        for j in range(k + 1):
            h[(j, k)] = dot(w, c[j])
            for i in range(j + 1):
                u[i] = u[i] - h[(j, k)] * c[j][i]
        norm = jnp.sqrt(jnp.maximum(dot(u, u), 0.0) + EPSILON)
        h[(k + 1, k)] = norm
        c.append([v / norm for v in u])
    return c, h


def kernel(
    x_hbm, nb_hbm, rows_hbm, cols_hbm, mirror_hbm, q_ref, h_ref,
    x_ref, nb, rows_ref, cols_ref, mirror_ref,
    wina, winb, win1, win2, xs, xr, zs, zr, red0, red1, total_ref,
    load_sem, swap_send, swap_recv, middle_send, middle_recv, cross_send, cross_recv, halo_send, halo_recv,
    zx_send, zx_recv, red_send, red_recv, pass_send, pass_recv,
):
    side = lax.axis_index("side")
    grp = lax.axis_index("grp")
    dev = lax.axis_index("dev")
    owner = grp * N_DEV + dev
    is_port = side == 0
    chip_x, y_lo, core = dev // 8, (dev // 2) % 4, dev % 2
    is_early = grp < EARLY
    is_edge = (owner < WIN) | (owner >= N_OWNERS - WIN)
    column = grp * 2 + core
    spot = chip_x * 8 + side * 4 + y_lo

    def exists(distance):
        return (owner + distance >= 0) & (owner + distance < N_OWNERS)

    partner = (1 - side, grp, dev)

    def near(distance, across):
        other = owner + distance
        return (1 - side if across else side, other // N_DEV, other % N_DEV)

    def in_column(flip, half):
        return (side, half + (grp % EARLY ^ (flip // 2)), chip_x * 8 + y_lo * 2 + (core ^ (flip % 2)))

    def in_plane(flip):
        other = spot ^ flip
        return ((other // 4) % 2, grp, (other // 8) * 8 + (other % 4) * 2 + core)

    def for_each(items, act, forward=True):
        @pl.when(jnp.logical_not(is_edge))
        def _():
            for _, item in items:
                act(item)

        @pl.when(is_edge)
        def _():
            for d, item in items:

                @pl.when(exists(d if forward else -d))
                def _(item=item):
                    act(item)

    barrier = pltpu.get_barrier_semaphore()

    def greet(device):
        pl.semaphore_signal(barrier, inc=1, device_id=device, device_id_type=MESH)

    neighbours = [(d, near(d, across)) for d in DISTANCES for across in (False, True)]
    greet(partner)
    for_each(neighbours, greet)

    @pl.when(is_early)
    def _():
        for flip in FLIPS:
            greet(in_plane(flip))
        for flip in range(1, 8):
            greet(in_column(flip, 0))
        for flip in range(8):
            greet(in_column(flip, EARLY))

    loads = [
        pltpu.make_async_copy(source, target, load_sem.at[n])
        for n, (source, target) in enumerate(
            (
                (x_hbm, x_ref),
                (mirror_hbm, mirror_ref),
                (cols_hbm, cols_ref),
                (rows_hbm, rows_ref),
                (nb_hbm.at[0], nb),
            )
        )
    ]
    for load in loads:
        load.start()
    loads[0].wait()
    loads[1].wait()

    index = [
        jnp.broadcast_to(mirror_ref[b : b + 1, :], (NRHS, BLOCK)) for b in range(BLK_DEV)
    ]
    own = [x_ref[0, :, b * BLOCK : (b + 1) * BLOCK] for b in range(BLK_DEV)]
    star = [lane_gather(own[b], index[b]) for b in range(BLK_DEV)]
    for b in range(BLK_DEV):
        sent = jnp.where(is_port, own[b], star[b])
        xs[b] = sent
        wina[OWN + b] = sent.astype(jnp.bfloat16)

    present = 1
    for d in DISTANCES:
        present = present + 2 * exists(d).astype(jnp.int32)
    pl.semaphore_wait(barrier, present + jnp.where(is_early, len(FLIPS) + 7, 8))

    def remote(source, target, send_sem, recv_sem, device):
        return pltpu.make_async_remote_copy(
            src_ref=source, dst_ref=target, send_sem=send_sem, recv_sem=recv_sem,
            device_id=device, device_id_type=MESH,
        )

    def start(copy):
        copy.start()

    def received(copy):
        copy.wait_recv()

    def sent_off(copy):
        copy.wait_send()

    swap = remote(xs, xr, swap_send, swap_recv, partner)
    copies, hop_copies = [swap], []

    def halo(window, target, across, send_sem, recv_sem, distances):
        return [
            (
                d,
                remote(
                    window.at[pl.ds(OWN, BLK_DEV)],
                    target.at[pl.ds((WIN - d) * BLK_DEV, BLK_DEV)],
                    send_sem.at[WIN + d], recv_sem.at[WIN + d], near(d, across),
                ),
            )
            for d in distances
        ]

    outward = jnp.where(y_lo >= 2, 1, -1)
    far_first = [outward * d for d in range(WIN, 0, -1)]
    near_last = [outward * -d for d in range(WIN, 0, -1)]

    middle = remote(
        wina.at[pl.ds(OWN, BLK_DEV)], winb.at[pl.ds(OWN, BLK_DEV)], middle_send, middle_recv, partner
    )
    start(middle)
    copies.append(middle)

    def over_there(distances):
        return halo(wina, winb, True, cross_send, cross_recv, distances)

    def over_here(distances):
        return halo(wina, wina, False, halo_send.at[0], halo_recv.at[0], distances)

    for_each(
        over_there([1, -1]) + over_here(far_first) + over_there([2, -2, 3, -3, 4, -4])
        + over_here(near_last),
        start,
    )
    hops = over_there(DISTANCES) + over_here(DISTANCES)
    start(swap)
    hop_copies += hops

    inverse = []
    for b in range(BLK_DEV):
        where_to = lax.broadcasted_iota(jnp.int32, (BLOCK, BLOCK), 0)
        onehot = jnp.where(
            jnp.broadcast_to(mirror_ref[b : b + 1, :], (BLOCK, BLOCK)) == where_to, 1.0, 0.0
        ).astype(jnp.bfloat16)
        lanes = lax.broadcasted_iota(jnp.int32, (16, BLOCK), 1).astype(jnp.float32).astype(jnp.bfloat16)
        found = lax.dot_general(
            lanes, onehot, (((1,), (1,)), ((), ())), preferred_element_type=jnp.float32
        )
        inverse.append(found[:NRHS].astype(jnp.int32))

    lane = lax.broadcasted_iota(jnp.int32, (NRHS, BLOCK), 1)
    sublane = lax.broadcasted_iota(jnp.int32, (NRHS, BLOCK), 0)
    sign = jnp.where(is_port, 1.0, -1.0)

    z = [[None] * BLK_DEV for _ in range(ITERS + 1)]
    for load in loads[2:]:
        load.wait()
    where_from = [
        jnp.clip(cols_ref[0, e] - (owner - WIN) * BLK_DEV, 0, SLOTS - 1) for e in range(NB_DEV)
    ]
    upper = [(rows_ref[0, e] == 0).astype(jnp.float32) for e in range(NB_DEV)]

    for e in range(NB_DEV):
        nb[e] = jnp.transpose(nb[e])

    def products(windows):
        total = jnp.zeros((16 * len(windows), BLOCK), jnp.float32)
        for e in range(0, NB_DEV, 2):
            lefts, rights = [], []
            for f in (e, e + 1):
                parts = []
                for window in windows:
                    picked = window[where_from[f]].astype(jnp.float32)
                    parts += [picked * upper[f], picked * (1.0 - upper[f])]
                lefts.append(jnp.concatenate(parts, axis=0).astype(jnp.bfloat16))
                rights.append(nb[f])
            total = total + lax.dot_general(
                jnp.concatenate(lefts, axis=1),
                jnp.concatenate(rights, axis=0),
                (((1,), (0,)), ((), ())),
                preferred_element_type=jnp.float32,
            )
        return total

    exchanged = []
    for k in range(ITERS):
        if k > 0:
            window = (None, win1, win2)[k]
            for b in range(BLK_DEV):
                window[OWN + b] = z[k][b].astype(jnp.bfloat16)
            for_each(
                halo(window, window, False, halo_send.at[k], halo_recv.at[k], far_first + near_last),
                start,
            )
            hops = halo(window, window, False, halo_send.at[k], halo_recv.at[k], DISTANCES)
            hop_copies += hops
            for b in range(BLK_DEV):
                zs[k - 1, b] = z[k][b]
            exchanged.append(
                remote(zs.at[k - 1], zr.at[k - 1], zx_send.at[k - 1], zx_recv.at[k - 1], partner)
            )
            start(exchanged[-1])
        for_each(hops, received, forward=False)
        if k == 0:
            received(middle)
            total = products([wina, winb])
            total = sign * total[:16] + total[16:]
        else:
            total = products([window])
        z[k + 1] = [total[:NRHS], total[NRHS:]]

    received(swap)
    for b in range(BLK_DEV):
        z[0][b] = xr[b] + sign * xs[b]
    partial = jnp.zeros((NRHS, BLOCK), jnp.float32)
    for p, (i, j) in enumerate(PAIRS):
        product = z[i][0] * z[j][0] + z[i][1] * z[j][1]
        partial = jnp.where(
            lane == p * NRHS + sublane, jnp.sum(product, axis=1, keepdims=True), partial
        )
    row = jnp.sum(partial, axis=0, keepdims=True)

    def total_of(red, size):
        parts = [red[n] for n in range(size)]
        while len(parts) > 1:
            parts = [a + b for a, b in zip(parts[::2], parts[1::2], strict=True)]
        return parts[0]

    red0[column] = row

    def to_column(flip, is_late):
        kind = 8 * is_late + flip
        return remote(
            red0.at[column], red0.at[column], red_send.at[flip], red_recv.at[0, kind], in_column(flip, 0)
        )

    early_copies = [to_column(flip, 0) for flip in range(8)]
    late_copies = [to_column(flip, 1) for flip in range(8)]

    @pl.when(is_early)
    def _():
        for copy in early_copies[1:]:
            start(copy)

    @pl.when(jnp.logical_not(is_early))
    def _():
        for copy in late_copies:
            start(copy)

    for b in range(BLK_DEV):
        zs[ITERS - 1, b] = z[ITERS][b]
    exchanged.append(
        remote(
            zs.at[ITERS - 1], zr.at[ITERS - 1], zx_send.at[ITERS - 1], zx_recv.at[ITERS - 1], partner
        )
    )
    start(exchanged[-1])
    copies += exchanged

    plane_copies = [
        remote(red1.at[spot], red1.at[spot], red_send.at[flip], red_recv.at[1, flip], in_plane(flip))
        for flip in FLIPS
    ]
    pass_on = remote(
        total_ref, total_ref, pass_send, pass_recv, (side, grp % EARLY + EARLY, dev)
    )

    @pl.when(is_early)
    def _():
        for copy in early_copies[1:] + late_copies:
            received(copy)
        for copy in early_copies[1:]:
            sent_off(copy)
        red1[spot] = total_of(red0, STAGE_SIZES[0])
        for copy in plane_copies:
            start(copy)

    images = [own]
    for k in range(ITERS):
        received(exchanged[k])
        image = []
        for b in range(BLK_DEV):
            mine, other = z[k + 1][b], zr[k, b]
            port = 0.5 * (mine + other)
            starboard = lane_gather(0.5 * (other - mine), inverse[b])
            image.append(jnp.where(is_port, port, starboard))
        images.append(image)

    @pl.when(is_early)
    def _():
        for copy in plane_copies:
            received(copy)
        total_ref[...] = total_of(red1, STAGE_SIZES[1])
        start(pass_on)

    @pl.when(jnp.logical_not(is_early))
    def _():
        received(pass_on)

    row = total_ref[...]
    spread = jnp.broadcast_to(row * (0.5 / TOTAL_PANELS), (NRHS, BLOCK))
    gram = {}
    for p, pair in enumerate(PAIRS):
        chosen = jnp.where(lane == p * NRHS + sublane, spread, 0.0)
        gram[pair] = jnp.broadcast_to(jnp.sum(chosen, axis=1, keepdims=True), (NRHS, BLOCK))
    c, h = coefficients(gram)
    for j in range(ITERS + 1):
        for b in range(BLK_DEV):
            value = c[j][0] * images[0][b]
            for i in range(1, j + 1):
                value = value + c[j][i] * images[i][b]
            q_ref[j, 0, :, b * BLOCK : (b + 1) * BLOCK] = value
    table = jnp.zeros((NRHS, BLOCK), jnp.float32)
    for (j, k), value in h.items():
        table = jnp.where(lane == k * (ITERS + 1) + j, value, table)
    turned = jnp.transpose(table)
    for k in range(ITERS):
        h_ref[k] = turned[k * (ITERS + 1) : (k + 1) * (ITERS + 1), :]
    for copy in copies:
        sent_off(copy)
    for_each(hop_copies, sent_off)

    @pl.when(is_early)
    def _():
        for copy in plane_copies:
            sent_off(copy)
        sent_off(pass_on)

    @pl.when(jnp.logical_not(is_early))
    def _():
        for copy in late_copies:
            sent_off(copy)


def settle(q_ref, h_ref, q_out, h_out, sem):
    moves = [
        pltpu.make_async_copy(q_ref, q_out, sem.at[0]),
        pltpu.make_async_copy(h_ref, h_out, sem.at[1]),
    ]
    for move in moves:
        move.start()
    for move in moves:
        move.wait()


def on_device(sources, near_blocks, block_rows, block_cols, mirror):
    vmem = pl.BlockSpec(memory_space=pltpu.VMEM)
    hbm = pl.BlockSpec(memory_space=pltpu.HBM)
    f32, bf16 = jnp.float32, jnp.bfloat16
    dma = pltpu.SemaphoreType.DMA
    window = pltpu.VMEM((SLOTS, NRHS, BLOCK), bf16)
    blocks = pltpu.VMEM((BLK_DEV, NRHS, BLOCK), f32)
    steps = pltpu.VMEM((ITERS, BLK_DEV, NRHS, BLOCK), f32)
    q, h = pl.pallas_call(
        kernel,
        out_shape=(
            jax.ShapeDtypeStruct((ITERS + 1, 1, NRHS, BLK_DEV * BLOCK), f32),
            jax.ShapeDtypeStruct((ITERS, ITERS + 1, NRHS), f32),
        ),
        in_specs=[hbm] * 5,
        out_specs=(vmem, vmem),
        scratch_shapes=[
            pltpu.VMEM((1, NRHS, BLK_DEV * BLOCK), f32),
            pltpu.VMEM((NB_DEV, BLOCK, BLOCK), bf16),
            pltpu.SMEM((1, NB_DEV), jnp.int32),
            pltpu.SMEM((1, NB_DEV), jnp.int32),
            pltpu.VMEM((BLK_DEV, BLOCK), jnp.int32),
            window, window, window, window,
            blocks, blocks,
            steps, steps,
            *[pltpu.VMEM((size, 1, BLOCK), f32) for size in STAGE_SIZES],
            pltpu.VMEM((1, BLOCK), f32),
            dma((5,)),
            dma, dma,
            dma, dma,
            dma((2 * WIN + 1,)), dma((2 * WIN + 1,)),
            dma((ITERS, 2 * WIN + 1)), dma((ITERS, 2 * WIN + 1)),
            dma((ITERS,)), dma((ITERS,)),
            dma((32,)), dma((2, 32)),
            dma, dma,
        ],
        compiler_params=pltpu.CompilerParams(
            collective_id=0, has_side_effects=True, vmem_limit_bytes=8 * 1024 * 1024
        ),
    )(
        *[
            pltpu.with_memory_space_constraint(operand, pltpu.HBM)
            for operand in (
                sources, near_blocks, block_rows, block_cols, mirror.reshape(BLK_DEV, BLOCK)
            )
        ]
    )
    q, h = pl.pallas_call(
        settle,
        out_shape=(
            jax.ShapeDtypeStruct(q.shape, f32),
            jax.ShapeDtypeStruct(h.shape, f32),
        ),
        in_specs=[vmem, vmem],
        out_specs=(hbm, hbm),
        scratch_shapes=[dma((2,))],
        compiler_params=pltpu.CompilerParams(vmem_limit_bytes=8 * 1024 * 1024),
    )(q, h)
    return q, jnp.transpose(h)


def solution(mesh):
    placed = (
        P("side", None, ("grp", "dev")),
        P("side", ("grp", "dev"), None, None),
        P("side", ("grp", "dev")),
        P("side", ("grp", "dev")),
        P(("grp", "dev")),
    )
    return jax.shard_map(
        on_device,
        mesh=mesh,
        in_specs=placed,
        out_specs=(P(None, "side", None, ("grp", "dev")), P()),
        check_vma=False,
    )
```

```python
import jax
import jax.numpy as jnp
from jax import lax
from jax.experimental import pallas as pl
from jax.experimental.pallas import tpu as pltpu
from jax.sharding import PartitionSpec as P

BLOCK = 128
BLK_DEV = 2
WIN = 4
ITERS = 3
NB_DEV = 32
NRHS = 8
N_GRP = 8
N_DEV = 32
TOTAL_PANELS = 131072.0
EPSILON = 1e-06
SLOTS = (2 * WIN + 1) * BLK_DEV
OWN = WIN * BLK_DEV
MESH = pl.DeviceIdType.MESH
PAIRS = [(i, j) for j in range(ITERS + 1) for i in range(j + 1)]
N_OWNERS = N_GRP * N_DEV
STAGE_SIZES = (16, 32)
EARLY = N_GRP // 2
X_HOPS = (0, 1, 2, 1)
Y_HOPS = (0, 1, 2, 3, 4, 3, 2, 3)
FLIPS = sorted(range(1, 32), key=lambda f: -X_HOPS[f // 8] - Y_HOPS[f % 8])
DISTANCES = [4, -4, 3, -3, 2, -2, 1, -1]


def lane_gather(x, index):
    return jnp.take_along_axis(x, index, axis=1, mode="promise_in_bounds")


def coefficients(gram):
    def dot(a, b):
        total = None
        for i, ai in enumerate(a):
            row = None
            for j, bj in enumerate(b):
                term = gram[(min(i, j), max(i, j))] * bj
                row = term if row is None else row + term
            total = ai * row if total is None else total + ai * row
        return total

    c = [[1.0 / jnp.sqrt(gram[(0, 0)] + EPSILON)]]
    h = {}
    for k in range(ITERS):
        w = [0.5 * v for v in c[k]] + [c[k][k]]
        for i in range(1, k + 1):
            w[i] = w[i] + c[k][i - 1]
        u = list(w)
        for j in range(k + 1):
            h[(j, k)] = dot(w, c[j])
            for i in range(j + 1):
                u[i] = u[i] - h[(j, k)] * c[j][i]
        norm = jnp.sqrt(jnp.maximum(dot(u, u), 0.0) + EPSILON)
        h[(k + 1, k)] = norm
        c.append([v / norm for v in u])
    return c, h


def kernel(
    x_hbm, nb_hbm, rows_hbm, cols_hbm, mirror_hbm, q_ref, h_ref,
    x_ref, nb, rows_ref, cols_ref, mirror_ref,
    wina, winb, win1, win2, xs, xr, zs, zr, red0, red1, total_ref,
    load_sem, swap_send, swap_recv, middle_send, middle_recv, cross_send, cross_recv, halo_send, halo_recv,
    zx_send, zx_recv, red_send, red_recv, pass_send, pass_recv,
):
    side = lax.axis_index("side")
    grp = lax.axis_index("grp")
    dev = lax.axis_index("dev")
    owner = grp * N_DEV + dev
    is_port = side == 0
    chip_x, y_lo, core = dev // 8, (dev // 2) % 4, dev % 2
    is_early = grp < EARLY
    is_edge = (owner < WIN) | (owner >= N_OWNERS - WIN)
    column = grp * 2 + core
    spot = chip_x * 8 + side * 4 + y_lo

    def exists(distance):
        return (owner + distance >= 0) & (owner + distance < N_OWNERS)

    partner = (1 - side, grp, dev)

    def near(distance, across):
        other = owner + distance
        return (1 - side if across else side, other // N_DEV, other % N_DEV)

    def in_column(flip, half):
        return (side, half + (grp % EARLY ^ (flip // 2)), chip_x * 8 + y_lo * 2 + (core ^ (flip % 2)))

    def in_plane(flip):
        other = spot ^ flip
        return ((other // 4) % 2, grp, (other // 8) * 8 + (other % 4) * 2 + core)

    def for_each(items, act, forward=True):
        @pl.when(jnp.logical_not(is_edge))
        def _():
            for _, item in items:
                act(item)

        @pl.when(is_edge)
        def _():
            for d, item in items:

                @pl.when(exists(d if forward else -d))
                def _(item=item):
                    act(item)

    barrier = pltpu.get_barrier_semaphore()

    def greet(device):
        pl.semaphore_signal(barrier, inc=1, device_id=device, device_id_type=MESH)

    neighbours = [(d, near(d, across)) for d in DISTANCES for across in (False, True)]
    greet(partner)
    for_each(neighbours, greet)

    @pl.when(is_early)
    def _():
        for flip in FLIPS:
            greet(in_plane(flip))
        for flip in range(1, 8):
            greet(in_column(flip, 0))
        for flip in range(8):
            greet(in_column(flip, EARLY))

    loads = [
        pltpu.make_async_copy(source, target, load_sem.at[n])
        for n, (source, target) in enumerate(
            (
                (x_hbm, x_ref),
                (mirror_hbm, mirror_ref),
                (cols_hbm, cols_ref),
                (rows_hbm, rows_ref),
                (nb_hbm.at[0], nb),
            )
        )
    ]
    for load in loads:
        load.start()
    loads[0].wait()
    loads[1].wait()

    index = [
        jnp.broadcast_to(mirror_ref[b : b + 1, :], (NRHS, BLOCK)) for b in range(BLK_DEV)
    ]
    own = [x_ref[0, :, b * BLOCK : (b + 1) * BLOCK] for b in range(BLK_DEV)]
    star = [lane_gather(own[b], index[b]) for b in range(BLK_DEV)]
    for b in range(BLK_DEV):
        sent = jnp.where(is_port, own[b], star[b])
        xs[b] = sent
        wina[OWN + b] = sent.astype(jnp.bfloat16)

    present = 1
    for d in DISTANCES:
        present = present + 2 * exists(d).astype(jnp.int32)
    pl.semaphore_wait(barrier, present + jnp.where(is_early, len(FLIPS) + 7, 8))

    def remote(source, target, send_sem, recv_sem, device):
        return pltpu.make_async_remote_copy(
            src_ref=source, dst_ref=target, send_sem=send_sem, recv_sem=recv_sem,
            device_id=device, device_id_type=MESH,
        )

    def start(copy):
        copy.start()

    def received(copy):
        copy.wait_recv()

    def sent_off(copy):
        copy.wait_send()

    swap = remote(xs, xr, swap_send, swap_recv, partner)
    copies, hop_copies = [swap], []

    def halo(window, target, across, send_sem, recv_sem, distances):
        return [
            (
                d,
                remote(
                    window.at[pl.ds(OWN, BLK_DEV)],
                    target.at[pl.ds((WIN - d) * BLK_DEV, BLK_DEV)],
                    send_sem.at[WIN + d], recv_sem.at[WIN + d], near(d, across),
                ),
            )
            for d in distances
        ]

    outward = jnp.where(y_lo >= 2, 1, -1)
    far_first = [outward * d for d in range(WIN, 0, -1)]
    near_last = [outward * -d for d in range(WIN, 0, -1)]

    middle = remote(
        wina.at[pl.ds(OWN, BLK_DEV)], winb.at[pl.ds(OWN, BLK_DEV)], middle_send, middle_recv, partner
    )
    start(middle)
    copies.append(middle)

    def over_there(distances):
        return halo(wina, winb, True, cross_send, cross_recv, distances)

    def over_here(distances):
        return halo(wina, wina, False, halo_send.at[0], halo_recv.at[0], distances)

    for_each(
        over_there([1, -1]) + over_here(far_first) + over_there([2, -2, 3, -3, 4, -4])
        + over_here(near_last),
        start,
    )
    hops = over_there(DISTANCES) + over_here(DISTANCES)
    start(swap)
    hop_copies += hops

    inverse = []
    for b in range(BLK_DEV):
        where_to = lax.broadcasted_iota(jnp.int32, (BLOCK, BLOCK), 0)
        onehot = jnp.where(
            jnp.broadcast_to(mirror_ref[b : b + 1, :], (BLOCK, BLOCK)) == where_to, 1.0, 0.0
        ).astype(jnp.bfloat16)
        lanes = lax.broadcasted_iota(jnp.int32, (16, BLOCK), 1).astype(jnp.float32).astype(jnp.bfloat16)
        found = lax.dot_general(
            lanes, onehot, (((1,), (1,)), ((), ())), preferred_element_type=jnp.float32
        )
        inverse.append(found[:NRHS].astype(jnp.int32))

    lane = lax.broadcasted_iota(jnp.int32, (NRHS, BLOCK), 1)
    sublane = lax.broadcasted_iota(jnp.int32, (NRHS, BLOCK), 0)
    sign = jnp.where(is_port, 1.0, -1.0)

    z = [[None] * BLK_DEV for _ in range(ITERS + 1)]
    for load in loads[2:]:
        load.wait()
    where_from = [
        jnp.clip(cols_ref[0, e] - (owner - WIN) * BLK_DEV, 0, SLOTS - 1) for e in range(NB_DEV)
    ]
    upper = [(rows_ref[0, e] == 0).astype(jnp.float32) for e in range(NB_DEV)]

    for e in range(NB_DEV):
        nb[e] = jnp.transpose(nb[e])

    def products(windows):
        total = jnp.zeros((16 * len(windows), BLOCK), jnp.float32)
        for e in range(0, NB_DEV, 2):
            lefts, rights = [], []
            for f in (e, e + 1):
                parts = []
                for window in windows:
                    picked = window[where_from[f]].astype(jnp.float32)
                    parts += [picked * upper[f], picked * (1.0 - upper[f])]
                lefts.append(jnp.concatenate(parts, axis=0).astype(jnp.bfloat16))
                rights.append(nb[f])
            total = total + lax.dot_general(
                jnp.concatenate(lefts, axis=1),
                jnp.concatenate(rights, axis=0),
                (((1,), (0,)), ((), ())),
                preferred_element_type=jnp.float32,
            )
        return total

    def with_pairs(partial, pairs):
        for i, j in pairs:
            product = z[i][0] * z[j][0] + z[i][1] * z[j][1]
            partial = jnp.where(
                lane == PAIRS.index((i, j)) * NRHS + sublane,
                jnp.sum(product, axis=1, keepdims=True),
                partial,
            )
        return partial

    exchanged = []
    for k in range(ITERS):
        if k > 0:
            window = (None, win1, win2)[k]
            for b in range(BLK_DEV):
                window[OWN + b] = z[k][b].astype(jnp.bfloat16)
            for_each(
                halo(window, window, False, halo_send.at[k], halo_recv.at[k], far_first + near_last),
                start,
            )
            hops = halo(window, window, False, halo_send.at[k], halo_recv.at[k], DISTANCES)
            hop_copies += hops
            for b in range(BLK_DEV):
                zs[k - 1, b] = z[k][b]
            exchanged.append(
                remote(zs.at[k - 1], zr.at[k - 1], zx_send.at[k - 1], zx_recv.at[k - 1], partner)
            )
            start(exchanged[-1])
        if k == ITERS - 1:
            received(swap)
            for b in range(BLK_DEV):
                z[0][b] = xr[b] + sign * xs[b]
            partial = with_pairs(
                jnp.zeros((NRHS, BLOCK), jnp.float32), [p for p in PAIRS if p[1] < ITERS]
            )
        for_each(hops, received, forward=False)
        if k == 0:
            received(middle)
            total = products([wina, winb])
            total = sign * total[:16] + total[16:]
        else:
            total = products([window])
        z[k + 1] = [total[:NRHS], total[NRHS:]]

    partial = with_pairs(partial, [p for p in PAIRS if p[1] == ITERS])
    row = jnp.sum(partial, axis=0, keepdims=True)

    def total_of(red, size):
        parts = [red[n] for n in range(size)]
        while len(parts) > 1:
            parts = [a + b for a, b in zip(parts[::2], parts[1::2], strict=True)]
        return parts[0]

    red0[column] = row

    def to_column(flip, is_late):
        kind = 8 * is_late + flip
        return remote(
            red0.at[column], red0.at[column], red_send.at[flip], red_recv.at[0, kind], in_column(flip, 0)
        )

    early_copies = [to_column(flip, 0) for flip in range(8)]
    late_copies = [to_column(flip, 1) for flip in range(8)]

    @pl.when(is_early)
    def _():
        for copy in early_copies[1:]:
            start(copy)

    @pl.when(jnp.logical_not(is_early))
    def _():
        for z_to in range(EARLY):
            for core_flip in range(2):
                start(to_column((grp % EARLY ^ z_to) * 2 + core_flip, 1))

    for b in range(BLK_DEV):
        zs[ITERS - 1, b] = z[ITERS][b]
    exchanged.append(
        remote(
            zs.at[ITERS - 1], zr.at[ITERS - 1], zx_send.at[ITERS - 1], zx_recv.at[ITERS - 1], partner
        )
    )
    start(exchanged[-1])
    copies += exchanged

    def to_plane(flip):
        return remote(
            red1.at[spot], red1.at[spot], red_send.at[flip], red_recv.at[1, flip], in_plane(flip)
        )

    plane_copies = [to_plane(flip) for flip in range(1, 32)]

    passes = grp == EARLY - 1
    pass_on = [
        remote(total_ref, total_ref, pass_send.at[n], pass_recv, (side, EARLY + n, dev))
        for n in range(N_GRP - EARLY)
    ]

    @pl.when(is_early)
    def _():
        for copy in early_copies[1:] + late_copies:
            received(copy)
        for copy in early_copies[1:]:
            sent_off(copy)
        red1[spot] = total_of(red0, STAGE_SIZES[0])
        for y_to in (0, 1, 2, 3, 7, 4, 5, 6):
            y_flip = spot % 8 ^ y_to
            for x_flip in (2, 1, 3):
                start(to_plane(x_flip * 8 + y_flip))

            @pl.when(y_flip > 0)
            def _(y_flip=y_flip):
                start(to_plane(y_flip))


    images = [own]
    for k in range(ITERS):
        received(exchanged[k])
        image = []
        for b in range(BLK_DEV):
            mine, other = z[k + 1][b], zr[k, b]
            port = 0.5 * (mine + other)
            starboard = lane_gather(0.5 * (other - mine), inverse[b])
            image.append(jnp.where(is_port, port, starboard))
        images.append(image)

    @pl.when(is_early)
    def _():
        for copy in plane_copies:
            received(copy)
        total_ref[...] = total_of(red1, STAGE_SIZES[1])

    @pl.when(passes)
    def _():
        for copy in pass_on:
            start(copy)

    @pl.when(jnp.logical_not(is_early))
    def _():
        received(pass_on[0])

    row = total_ref[...]
    spread = jnp.broadcast_to(row * (0.5 / TOTAL_PANELS), (NRHS, BLOCK))
    gram = {}
    for p, pair in enumerate(PAIRS):
        chosen = jnp.where(lane == p * NRHS + sublane, spread, 0.0)
        gram[pair] = jnp.broadcast_to(jnp.sum(chosen, axis=1, keepdims=True), (NRHS, BLOCK))
    c, h = coefficients(gram)
    for j in range(ITERS + 1):
        for b in range(BLK_DEV):
            value = c[j][0] * images[0][b]
            for i in range(1, j + 1):
                value = value + c[j][i] * images[i][b]
            q_ref[j, 0, :, b * BLOCK : (b + 1) * BLOCK] = value
    table = jnp.zeros((NRHS, BLOCK), jnp.float32)
    for (j, k), value in h.items():
        table = jnp.where(lane == k * (ITERS + 1) + j, value, table)
    turned = jnp.transpose(table)
    for k in range(ITERS):
        h_ref[k] = turned[k * (ITERS + 1) : (k + 1) * (ITERS + 1), :]
    for copy in copies:
        sent_off(copy)
    for_each(hop_copies, sent_off)

    @pl.when(is_early)
    def _():
        for copy in plane_copies:
            sent_off(copy)

    @pl.when(passes)
    def _():
        for copy in pass_on:
            sent_off(copy)

    @pl.when(jnp.logical_not(is_early))
    def _():
        for copy in late_copies:
            sent_off(copy)


def settle(q_ref, h_ref, q_out, h_out, sem):
    moves = [
        pltpu.make_async_copy(q_ref, q_out, sem.at[0]),
        pltpu.make_async_copy(h_ref, h_out, sem.at[1]),
    ]
    for move in moves:
        move.start()
    for move in moves:
        move.wait()


def on_device(sources, near_blocks, block_rows, block_cols, mirror):
    vmem = pl.BlockSpec(memory_space=pltpu.VMEM)
    hbm = pl.BlockSpec(memory_space=pltpu.HBM)
    f32, bf16 = jnp.float32, jnp.bfloat16
    dma = pltpu.SemaphoreType.DMA
    window = pltpu.VMEM((SLOTS, NRHS, BLOCK), bf16)
    blocks = pltpu.VMEM((BLK_DEV, NRHS, BLOCK), f32)
    steps = pltpu.VMEM((ITERS, BLK_DEV, NRHS, BLOCK), f32)
    q, h = pl.pallas_call(
        kernel,
        out_shape=(
            jax.ShapeDtypeStruct((ITERS + 1, 1, NRHS, BLK_DEV * BLOCK), f32),
            jax.ShapeDtypeStruct((ITERS, ITERS + 1, NRHS), f32),
        ),
        in_specs=[hbm] * 5,
        out_specs=(vmem, vmem),
        scratch_shapes=[
            pltpu.VMEM((1, NRHS, BLK_DEV * BLOCK), f32),
            pltpu.VMEM((NB_DEV, BLOCK, BLOCK), bf16),
            pltpu.SMEM((1, NB_DEV), jnp.int32),
            pltpu.SMEM((1, NB_DEV), jnp.int32),
            pltpu.VMEM((BLK_DEV, BLOCK), jnp.int32),
            window, window, window, window,
            blocks, blocks,
            steps, steps,
            *[pltpu.VMEM((size, 1, BLOCK), f32) for size in STAGE_SIZES],
            pltpu.VMEM((1, BLOCK), f32),
            dma((5,)),
            dma, dma,
            dma, dma,
            dma((2 * WIN + 1,)), dma((2 * WIN + 1,)),
            dma((ITERS, 2 * WIN + 1)), dma((ITERS, 2 * WIN + 1)),
            dma((ITERS,)), dma((ITERS,)),
            dma((32,)), dma((2, 32)),
            dma((N_GRP - EARLY,)), dma,
        ],
        compiler_params=pltpu.CompilerParams(
            collective_id=0, has_side_effects=True, vmem_limit_bytes=8 * 1024 * 1024
        ),
    )(
        *[
            pltpu.with_memory_space_constraint(operand, pltpu.HBM)
            for operand in (
                sources, near_blocks, block_rows, block_cols, mirror.reshape(BLK_DEV, BLOCK)
            )
        ]
    )
    q, h = pl.pallas_call(
        settle,
        out_shape=(
            jax.ShapeDtypeStruct(q.shape, f32),
            jax.ShapeDtypeStruct(h.shape, f32),
        ),
        in_specs=[vmem, vmem],
        out_specs=(hbm, hbm),
        scratch_shapes=[dma((2,))],
        compiler_params=pltpu.CompilerParams(vmem_limit_bytes=8 * 1024 * 1024),
    )(q, h)
    return q, jnp.transpose(h)


def solution(mesh):
    placed = (
        P("side", None, ("grp", "dev")),
        P("side", ("grp", "dev"), None, None),
        P("side", ("grp", "dev")),
        P("side", ("grp", "dev")),
        P(("grp", "dev")),
    )
    return jax.shard_map(
        on_device,
        mesh=mesh,
        in_specs=placed,
        out_specs=(P(None, "side", None, ("grp", "dev")), P()),
        check_vma=False,
    )
```

```python
import jax
import jax.numpy as jnp
from jax import lax
from jax.experimental import pallas as pl
from jax.experimental.pallas import tpu as pltpu
from jax.sharding import PartitionSpec as P

BLOCK = 128
BLK_DEV = 2
WIN = 4
ITERS = 3
NB_DEV = 32
NRHS = 8
N_GRP = 8
N_DEV = 32
TOTAL_PANELS = 131072.0
EPSILON = 1e-06
SLOTS = (2 * WIN + 1) * BLK_DEV
OWN = WIN * BLK_DEV
MESH = pl.DeviceIdType.MESH
PAIRS = [(i, j) for j in range(ITERS + 1) for i in range(j + 1)]
N_OWNERS = N_GRP * N_DEV
STAGE_SIZES = (16, 32)
EARLY = N_GRP // 2
X_HOPS = (0, 1, 2, 1)
Y_HOPS = (0, 1, 2, 3, 4, 3, 2, 3)
FLIPS = sorted(range(1, 32), key=lambda f: -X_HOPS[f // 8] - Y_HOPS[f % 8])
DISTANCES = [4, -4, 3, -3, 2, -2, 1, -1]


def lane_gather(x, index):
    return jnp.take_along_axis(x, index, axis=1, mode="promise_in_bounds")


def coefficients(gram):
    def dot(a, b):
        total = None
        for i, ai in enumerate(a):
            row = None
            for j, bj in enumerate(b):
                term = gram[(min(i, j), max(i, j))] * bj
                row = term if row is None else row + term
            total = ai * row if total is None else total + ai * row
        return total

    c = [[1.0 / jnp.sqrt(gram[(0, 0)] + EPSILON)]]
    h = {}
    for k in range(ITERS):
        w = [0.5 * v for v in c[k]] + [c[k][k]]
        for i in range(1, k + 1):
            w[i] = w[i] + c[k][i - 1]
        u = list(w)
        for j in range(k + 1):
            h[(j, k)] = dot(w, c[j])
            for i in range(j + 1):
                u[i] = u[i] - h[(j, k)] * c[j][i]
        norm = jnp.sqrt(jnp.maximum(dot(u, u), 0.0) + EPSILON)
        h[(k + 1, k)] = norm
        c.append([v / norm for v in u])
    return c, h


def kernel(
    x_hbm, nb_hbm, rows_hbm, cols_hbm, mirror_hbm, q_ref, h_ref,
    x_ref, nb, rows_ref, cols_ref, mirror_ref,
    wina, winb, win1, win2, xs, xr, zs, zr, red0, red1, total_ref,
    load_sem, swap_send, swap_recv, cross_send, cross_recv, halo_send, halo_recv,
    zx_send, zx_recv, red_send, red_recv, pass_send, pass_recv,
):
    side = lax.axis_index("side")
    grp = lax.axis_index("grp")
    dev = lax.axis_index("dev")
    owner = grp * N_DEV + dev
    is_port = side == 0
    chip_x, y_lo, core = dev // 8, (dev // 2) % 4, dev % 2
    is_early = grp < EARLY
    is_edge = (owner < WIN) | (owner >= N_OWNERS - WIN)
    column = grp * 2 + core
    spot = chip_x * 8 + side * 4 + y_lo

    def exists(distance):
        return (owner + distance >= 0) & (owner + distance < N_OWNERS)

    partner = (1 - side, grp, dev)

    def near(distance, across):
        other = owner + distance
        return (1 - side if across else side, other // N_DEV, other % N_DEV)

    def in_column(flip, half):
        return (side, half + (grp % EARLY ^ (flip // 2)), chip_x * 8 + y_lo * 2 + (core ^ (flip % 2)))

    def in_plane(flip):
        other = spot ^ flip
        return ((other // 4) % 2, grp, (other // 8) * 8 + (other % 4) * 2 + core)

    def for_each(items, act):
        @pl.when(jnp.logical_not(is_edge))
        def _():
            for _, item in items:
                act(item)

        @pl.when(is_edge)
        def _():
            for d, item in items:

                @pl.when(exists(d))
                def _(item=item):
                    act(item)

    n_near = 0
    for d in DISTANCES:
        n_near = n_near + exists(d).astype(jnp.int32)

    def wait_bytes(ref, count, sem):
        part = ref.at[pl.ds(0, count)]
        pltpu.make_async_copy(part, part, sem).wait()

    def wait_near(ref, sem, extra=0):
        @pl.when(jnp.logical_not(is_edge))
        def _():
            wait_bytes(ref, (2 * WIN + extra) * BLK_DEV, sem)

        @pl.when(is_edge)
        def _():
            for m in range(WIN, 2 * WIN):

                @pl.when(n_near == m)
                def _(m=m):
                    wait_bytes(ref, (m + extra) * BLK_DEV, sem)

    barrier = pltpu.get_barrier_semaphore()

    def greet(device):
        pl.semaphore_signal(barrier, inc=1, device_id=device, device_id_type=MESH)

    neighbours = [(d, near(d, across)) for d in DISTANCES for across in (False, True)]
    greet(partner)
    for_each(neighbours, greet)

    @pl.when(is_early)
    def _():
        for flip in FLIPS:
            greet(in_plane(flip))
        for flip in range(1, 8):
            greet(in_column(flip, 0))
        for flip in range(8):
            greet(in_column(flip, EARLY))

    loads = [
        pltpu.make_async_copy(source, target, load_sem.at[n])
        for n, (source, target) in enumerate(
            (
                (x_hbm, x_ref),
                (mirror_hbm, mirror_ref),
                (cols_hbm, cols_ref),
                (rows_hbm, rows_ref),
                (nb_hbm.at[0], nb),
            )
        )
    ]
    for load in loads:
        load.start()
    loads[0].wait()
    loads[1].wait()

    index = [
        jnp.broadcast_to(mirror_ref[b : b + 1, :], (NRHS, BLOCK)) for b in range(BLK_DEV)
    ]
    own = [x_ref[0, :, b * BLOCK : (b + 1) * BLOCK] for b in range(BLK_DEV)]
    star = [lane_gather(own[b], index[b]) for b in range(BLK_DEV)]
    for b in range(BLK_DEV):
        sent = jnp.where(is_port, own[b], star[b])
        xs[b] = sent
        wina[OWN + b] = sent.astype(jnp.bfloat16)

    pl.semaphore_wait(barrier, 1 + 2 * n_near + jnp.where(is_early, len(FLIPS) + 7, 8))

    def remote(source, target, send_sem, recv_sem, device):
        return pltpu.make_async_remote_copy(
            src_ref=source, dst_ref=target, send_sem=send_sem, recv_sem=recv_sem,
            device_id=device, device_id_type=MESH,
        )

    def start(copy):
        copy.start()

    def received(copy):
        copy.wait_recv()

    def sent_off(copy):
        copy.wait_send()

    swap = remote(xs, xr, swap_send, swap_recv, partner)
    copies = [swap]

    def halo(window, target, across, send_sem, recv_sem, distances):
        return [
            (
                d,
                remote(
                    window.at[pl.ds(OWN, BLK_DEV)],
                    target.at[pl.ds((WIN - d) * BLK_DEV, BLK_DEV)],
                    send_sem, recv_sem, near(d, across),
                ),
            )
            for d in distances
        ]

    outward = jnp.where(y_lo >= 2, 1, -1)
    far_first = [outward * d for d in range(WIN, 0, -1)]
    near_last = [outward * -d for d in range(WIN, 0, -1)]

    middle = remote(
        wina.at[pl.ds(OWN, BLK_DEV)], winb.at[pl.ds(OWN, BLK_DEV)], cross_send, cross_recv, partner
    )
    start(middle)

    def over_there(distances):
        return halo(wina, winb, True, cross_send, cross_recv, distances)

    def over_here(distances):
        return halo(wina, wina, False, halo_send.at[0], halo_recv.at[0], distances)

    for_each(
        over_there([1, -1]) + over_here(far_first) + over_there([2, -2, 3, -3, 4, -4])
        + over_here(near_last),
        start,
    )
    start(swap)

    inverse = []
    for b in range(BLK_DEV):
        where_to = lax.broadcasted_iota(jnp.int32, (BLOCK, BLOCK), 0)
        onehot = jnp.where(
            jnp.broadcast_to(mirror_ref[b : b + 1, :], (BLOCK, BLOCK)) == where_to, 1.0, 0.0
        ).astype(jnp.bfloat16)
        lanes = lax.broadcasted_iota(jnp.int32, (16, BLOCK), 1).astype(jnp.float32).astype(jnp.bfloat16)
        found = lax.dot_general(
            lanes, onehot, (((1,), (1,)), ((), ())), preferred_element_type=jnp.float32
        )
        inverse.append(found[:NRHS].astype(jnp.int32))

    lane = lax.broadcasted_iota(jnp.int32, (NRHS, BLOCK), 1)
    sublane = lax.broadcasted_iota(jnp.int32, (NRHS, BLOCK), 0)
    sign = jnp.where(is_port, 1.0, -1.0)

    z = [[None] * BLK_DEV for _ in range(ITERS + 1)]
    for load in loads[2:]:
        load.wait()
    where_from = [
        jnp.clip(cols_ref[0, e] - (owner - WIN) * BLK_DEV, 0, SLOTS - 1) for e in range(NB_DEV)
    ]
    upper = [(rows_ref[0, e] == 0).astype(jnp.float32) for e in range(NB_DEV)]

    for e in range(NB_DEV):
        nb[e] = jnp.transpose(nb[e])

    def products(windows):
        total = jnp.zeros((16 * len(windows), BLOCK), jnp.float32)
        for e in range(0, NB_DEV, 2):
            lefts, rights = [], []
            for f in (e, e + 1):
                parts = []
                for window in windows:
                    picked = window[where_from[f]].astype(jnp.float32)
                    parts += [picked * upper[f], picked * (1.0 - upper[f])]
                lefts.append(jnp.concatenate(parts, axis=0).astype(jnp.bfloat16))
                rights.append(nb[f])
            total = total + lax.dot_general(
                jnp.concatenate(lefts, axis=1),
                jnp.concatenate(rights, axis=0),
                (((1,), (0,)), ((), ())),
                preferred_element_type=jnp.float32,
            )
        return total

    def with_pairs(partial, pairs):
        for i, j in pairs:
            product = z[i][0] * z[j][0] + z[i][1] * z[j][1]
            partial = jnp.where(
                lane == PAIRS.index((i, j)) * NRHS + sublane,
                jnp.sum(product, axis=1, keepdims=True),
                partial,
            )
        return partial

    exchanged = []
    for k in range(ITERS):
        if k > 0:
            window = (None, win1, win2)[k]
            for b in range(BLK_DEV):
                window[OWN + b] = z[k][b].astype(jnp.bfloat16)
            for_each(
                halo(window, window, False, halo_send.at[k], halo_recv.at[k], far_first + near_last),
                start,
            )
            for b in range(BLK_DEV):
                zs[k - 1, b] = z[k][b]
            exchanged.append(
                remote(zs.at[k - 1], zr.at[k - 1], zx_send.at[k - 1], zx_recv.at[k - 1], partner)
            )
            start(exchanged[-1])
        if k == ITERS - 1:
            received(swap)
            for b in range(BLK_DEV):
                z[0][b] = xr[b] + sign * xs[b]
            partial = with_pairs(
                jnp.zeros((NRHS, BLOCK), jnp.float32), [p for p in PAIRS if p[1] < ITERS]
            )
        wait_near(wina if k == 0 else window, halo_recv.at[k])
        if k == 0:
            wait_near(winb, cross_recv, 1)
            total = products([wina, winb])
            total = sign * total[:16] + total[16:]
        else:
            total = products([window])
        z[k + 1] = [total[:NRHS], total[NRHS:]]

    partial = with_pairs(partial, [p for p in PAIRS if p[1] == ITERS])
    row = jnp.sum(partial, axis=0, keepdims=True)

    def total_of(red, size):
        parts = [red[n] for n in range(size)]
        while len(parts) > 1:
            parts = [a + b for a, b in zip(parts[::2], parts[1::2], strict=True)]
        return parts[0]

    red0[column] = row

    def to_column(flip):
        return remote(
            red0.at[column], red0.at[column], red_send.at[0], red_recv.at[0], in_column(flip, 0)
        )

    early_copies = [to_column(flip) for flip in range(8)]

    @pl.when(is_early)
    def _():
        for copy in early_copies[1:]:
            start(copy)

    @pl.when(jnp.logical_not(is_early))
    def _():
        for z_to in range(EARLY):
            for core_flip in range(2):
                start(to_column((grp % EARLY ^ z_to) * 2 + core_flip))

    for b in range(BLK_DEV):
        zs[ITERS - 1, b] = z[ITERS][b]
    exchanged.append(
        remote(
            zs.at[ITERS - 1], zr.at[ITERS - 1], zx_send.at[ITERS - 1], zx_recv.at[ITERS - 1], partner
        )
    )
    start(exchanged[-1])
    copies += exchanged

    def to_plane(flip):
        return remote(
            red1.at[spot], red1.at[spot], red_send.at[1], red_recv.at[1], in_plane(flip)
        )

    passes = grp == EARLY - 1
    pass_on = [
        remote(total_ref, total_ref, pass_send.at[n], pass_recv, (side, EARLY + n, dev))
        for n in range(N_GRP - EARLY)
    ]

    @pl.when(is_early)
    def _():
        wait_bytes(red0, STAGE_SIZES[0] - 1, red_recv.at[0])
        red1[spot] = total_of(red0, STAGE_SIZES[0])
        for y_to in (0, 1, 2, 3, 7, 4, 5, 6):
            y_flip = spot % 8 ^ y_to
            for x_flip in (2, 1, 3):
                start(to_plane(x_flip * 8 + y_flip))

            @pl.when(y_flip > 0)
            def _(y_flip=y_flip):
                start(to_plane(y_flip))


    images = [own]
    for k in range(ITERS):
        received(exchanged[k])
        image = []
        for b in range(BLK_DEV):
            mine, other = z[k + 1][b], zr[k, b]
            port = 0.5 * (mine + other)
            starboard = lane_gather(0.5 * (other - mine), inverse[b])
            image.append(jnp.where(is_port, port, starboard))
        images.append(image)

    for copy in copies:
        sent_off(copy)
    wait_near(winb, cross_send, 1)
    for k, window in enumerate((wina, win1, win2)):
        wait_near(window, halo_send.at[k])

    @pl.when(is_early)
    def _():
        wait_bytes(red0, 7, red_send.at[0])

    @pl.when(jnp.logical_not(is_early))
    def _():
        wait_bytes(red0, 8, red_send.at[0])

    @pl.when(is_early)
    def _():
        wait_bytes(red1, STAGE_SIZES[1] - 1, red_recv.at[1])
        total_ref[...] = total_of(red1, STAGE_SIZES[1])

    @pl.when(passes)
    def _():
        for copy in pass_on:
            start(copy)

    @pl.when(jnp.logical_not(is_early))
    def _():
        received(pass_on[0])

    row = total_ref[...]
    spread = jnp.broadcast_to(row * (0.5 / TOTAL_PANELS), (NRHS, BLOCK))
    gram = {}
    for p, pair in enumerate(PAIRS):
        chosen = jnp.where(lane == p * NRHS + sublane, spread, 0.0)
        gram[pair] = jnp.broadcast_to(jnp.sum(chosen, axis=1, keepdims=True), (NRHS, BLOCK))
    c, h = coefficients(gram)
    for j in range(ITERS + 1):
        for b in range(BLK_DEV):
            value = c[j][0] * images[0][b]
            for i in range(1, j + 1):
                value = value + c[j][i] * images[i][b]
            q_ref[j, 0, :, b * BLOCK : (b + 1) * BLOCK] = value
    table = jnp.zeros((NRHS, BLOCK), jnp.float32)
    for (j, k), value in h.items():
        table = jnp.where(lane == k * (ITERS + 1) + j, value, table)
    turned = jnp.transpose(table)
    for k in range(ITERS):
        h_ref[k] = turned[k * (ITERS + 1) : (k + 1) * (ITERS + 1), :]

    @pl.when(is_early)
    def _():
        wait_bytes(red1, STAGE_SIZES[1] - 1, red_send.at[1])

    @pl.when(passes)
    def _():
        for copy in pass_on:
            sent_off(copy)


def settle(q_ref, h_ref, q_out, h_out, sem):
    moves = [
        pltpu.make_async_copy(q_ref, q_out, sem.at[0]),
        pltpu.make_async_copy(h_ref, h_out, sem.at[1]),
    ]
    for move in moves:
        move.start()
    for move in moves:
        move.wait()


def on_device(sources, near_blocks, block_rows, block_cols, mirror):
    vmem = pl.BlockSpec(memory_space=pltpu.VMEM)
    hbm = pl.BlockSpec(memory_space=pltpu.HBM)
    f32, bf16 = jnp.float32, jnp.bfloat16
    dma = pltpu.SemaphoreType.DMA
    window = pltpu.VMEM((SLOTS, NRHS, BLOCK), bf16)
    blocks = pltpu.VMEM((BLK_DEV, NRHS, BLOCK), f32)
    steps = pltpu.VMEM((ITERS, BLK_DEV, NRHS, BLOCK), f32)
    q, h = pl.pallas_call(
        kernel,
        out_shape=(
            jax.ShapeDtypeStruct((ITERS + 1, 1, NRHS, BLK_DEV * BLOCK), f32),
            jax.ShapeDtypeStruct((ITERS, ITERS + 1, NRHS), f32),
        ),
        in_specs=[hbm] * 5,
        out_specs=(vmem, vmem),
        scratch_shapes=[
            pltpu.VMEM((1, NRHS, BLK_DEV * BLOCK), f32),
            pltpu.VMEM((NB_DEV, BLOCK, BLOCK), bf16),
            pltpu.SMEM((1, NB_DEV), jnp.int32),
            pltpu.SMEM((1, NB_DEV), jnp.int32),
            pltpu.VMEM((BLK_DEV, BLOCK), jnp.int32),
            window, window, window, window,
            blocks, blocks,
            steps, steps,
            *[pltpu.VMEM((size, 1, BLOCK), f32) for size in STAGE_SIZES],
            pltpu.VMEM((1, BLOCK), f32),
            dma((5,)),
            dma, dma,
            dma, dma,
            dma((ITERS,)), dma((ITERS,)),
            dma((ITERS,)), dma((ITERS,)),
            dma((2,)), dma((2,)),
            dma((N_GRP - EARLY,)), dma,
        ],
        compiler_params=pltpu.CompilerParams(
            collective_id=0, has_side_effects=True, vmem_limit_bytes=8 * 1024 * 1024
        ),
    )(
        *[
            pltpu.with_memory_space_constraint(operand, pltpu.HBM)
            for operand in (
                sources, near_blocks, block_rows, block_cols, mirror.reshape(BLK_DEV, BLOCK)
            )
        ]
    )
    q, h = pl.pallas_call(
        settle,
        out_shape=(
            jax.ShapeDtypeStruct(q.shape, f32),
            jax.ShapeDtypeStruct(h.shape, f32),
        ),
        in_specs=[vmem, vmem],
        out_specs=(hbm, hbm),
        scratch_shapes=[dma((2,))],
        compiler_params=pltpu.CompilerParams(vmem_limit_bytes=8 * 1024 * 1024),
    )(q, h)
    return q, jnp.transpose(h)


def solution(mesh):
    placed = (
        P("side", None, ("grp", "dev")),
        P("side", ("grp", "dev"), None, None),
        P("side", ("grp", "dev")),
        P("side", ("grp", "dev")),
        P(("grp", "dev")),
    )
    return jax.shard_map(
        on_device,
        mesh=mesh,
        in_specs=placed,
        out_specs=(P(None, "side", None, ("grp", "dev")), P()),
        check_vma=False,
    )
```

```python
import jax
import jax.numpy as jnp
from jax import lax
from jax.experimental import pallas as pl
from jax.experimental.pallas import tpu as pltpu
from jax.sharding import PartitionSpec as P

BLOCK = 128
BLK_DEV = 2
WIN = 4
ITERS = 3
NB_DEV = 32
NRHS = 8
N_GRP = 8
N_DEV = 32
TOTAL_PANELS = 131072.0
EPSILON = 1e-06
SLOTS = (2 * WIN + 1) * BLK_DEV
OWN = WIN * BLK_DEV
MESH = pl.DeviceIdType.MESH
PAIRS = [(i, j) for j in range(ITERS + 1) for i in range(j + 1)]
N_OWNERS = N_GRP * N_DEV
STAGE_SIZES = (16, 32)
EARLY = N_GRP // 2
X_HOPS = (0, 1, 2, 1)
Y_HOPS = (0, 1, 2, 3, 4, 3, 2, 3)
FLIPS = sorted(range(1, 32), key=lambda f: -X_HOPS[f // 8] - Y_HOPS[f % 8])
DISTANCES = [4, -4, 3, -3, 2, -2, 1, -1]


def lane_gather(x, index):
    return jnp.take_along_axis(x, index, axis=1, mode="promise_in_bounds")


def coefficients(gram):
    def dot(a, b):
        total = None
        for i, ai in enumerate(a):
            row = None
            for j, bj in enumerate(b):
                term = gram[(min(i, j), max(i, j))] * bj
                row = term if row is None else row + term
            total = ai * row if total is None else total + ai * row
        return total

    c = [[1.0 / jnp.sqrt(gram[(0, 0)] + EPSILON)]]
    h = {}
    for k in range(ITERS):
        w = [0.5 * v for v in c[k]] + [c[k][k]]
        for i in range(1, k + 1):
            w[i] = w[i] + c[k][i - 1]
        u = list(w)
        for j in range(k + 1):
            h[(j, k)] = dot(w, c[j])
            for i in range(j + 1):
                u[i] = u[i] - h[(j, k)] * c[j][i]
        norm = jnp.sqrt(jnp.maximum(dot(u, u), 0.0) + EPSILON)
        h[(k + 1, k)] = norm
        inverse = 1.0 / norm
        c.append([v * inverse for v in u])
    return c, h


def kernel(
    x_hbm, nb_hbm, rows_hbm, cols_hbm, mirror_hbm, q_ref, h_ref,
    x_ref, nb, rows_ref, cols_ref, mirror_ref,
    wina, winb, win1, win2, xs, xr, zs, zr, red0, red1, total_ref,
    load_sem, swap_send, swap_recv, cross_send, cross_recv, halo_send, halo_recv,
    zx_send, zx_recv, red_send, red_recv, pass_send, pass_recv,
):
    side = lax.axis_index("side")
    grp = lax.axis_index("grp")
    dev = lax.axis_index("dev")
    owner = grp * N_DEV + dev
    is_port = side == 0
    chip_x, y_lo, core = dev // 8, (dev // 2) % 4, dev % 2
    is_early = grp < EARLY
    is_edge = (owner < WIN) | (owner >= N_OWNERS - WIN)
    column = grp * 2 + core
    spot = chip_x * 8 + side * 4 + y_lo

    def exists(distance):
        return (owner + distance >= 0) & (owner + distance < N_OWNERS)

    partner = (1 - side, grp, dev)

    def near(distance, across):
        other = owner + distance
        return (1 - side if across else side, other // N_DEV, other % N_DEV)

    def in_column(flip, half):
        return (side, half + (grp % EARLY ^ (flip // 2)), chip_x * 8 + y_lo * 2 + (core ^ (flip % 2)))

    def in_plane(flip):
        other = spot ^ flip
        return ((other // 4) % 2, grp, (other // 8) * 8 + (other % 4) * 2 + core)

    def for_each(items, act):
        @pl.when(jnp.logical_not(is_edge))
        def _():
            for _, item in items:
                act(item)

        @pl.when(is_edge)
        def _():
            for d, item in items:

                @pl.when(exists(d))
                def _(item=item):
                    act(item)

    n_near = 0
    for d in DISTANCES:
        n_near = n_near + exists(d).astype(jnp.int32)

    def wait_bytes(ref, count, sem):
        part = ref.at[pl.ds(0, count)]
        pltpu.make_async_copy(part, part, sem).wait()

    def wait_near(ref, sem, extra=0):
        @pl.when(jnp.logical_not(is_edge))
        def _():
            wait_bytes(ref, (2 * WIN + extra) * BLK_DEV, sem)

        @pl.when(is_edge)
        def _():
            for m in range(WIN, 2 * WIN):

                @pl.when(n_near == m)
                def _(m=m):
                    wait_bytes(ref, (m + extra) * BLK_DEV, sem)

    loads = [
        pltpu.make_async_copy(source, target, load_sem.at[n])
        for n, (source, target) in enumerate(
            (
                (x_hbm, x_ref),
                (mirror_hbm, mirror_ref),
                (cols_hbm, cols_ref),
                (rows_hbm, rows_ref),
                (nb_hbm.at[0], nb),
            )
        )
    ]
    for load in loads:
        load.start()

    barrier = pltpu.get_barrier_semaphore()

    def greet(device):
        pl.semaphore_signal(barrier, inc=1, device_id=device, device_id_type=MESH)

    neighbours = [(d, near(d, across)) for d in DISTANCES for across in (False, True)]
    greet(partner)
    for_each(neighbours, greet)

    @pl.when(is_early)
    def _():
        for flip in FLIPS:
            greet(in_plane(flip))
        for flip in range(1, 8):
            greet(in_column(flip, 0))
        for flip in range(8):
            greet(in_column(flip, EARLY))

    loads[0].wait()
    loads[1].wait()

    index = [
        jnp.broadcast_to(mirror_ref[b : b + 1, :], (NRHS, BLOCK)) for b in range(BLK_DEV)
    ]
    own = [x_ref[0, :, b * BLOCK : (b + 1) * BLOCK] for b in range(BLK_DEV)]
    star = [lane_gather(own[b], index[b]) for b in range(BLK_DEV)]
    for b in range(BLK_DEV):
        sent = jnp.where(is_port, own[b], star[b])
        xs[b] = sent
        wina[OWN + b] = sent.astype(jnp.bfloat16)

    pl.semaphore_wait(barrier, 1 + 2 * n_near + jnp.where(is_early, len(FLIPS) + 7, 8))

    def remote(source, target, send_sem, recv_sem, device):
        return pltpu.make_async_remote_copy(
            src_ref=source, dst_ref=target, send_sem=send_sem, recv_sem=recv_sem,
            device_id=device, device_id_type=MESH,
        )

    def start(copy):
        copy.start()

    def received(copy):
        copy.wait_recv()

    def sent_off(copy):
        copy.wait_send()

    swap = remote(xs, xr, swap_send, swap_recv, partner)
    copies = [swap]

    def halo(window, target, across, send_sem, recv_sem, distances):
        return [
            (
                d,
                remote(
                    window.at[pl.ds(OWN, BLK_DEV)],
                    target.at[pl.ds((WIN - d) * BLK_DEV, BLK_DEV)],
                    send_sem, recv_sem, near(d, across),
                ),
            )
            for d in distances
        ]

    outward = jnp.where(y_lo >= 2, 1, -1)
    far_first = [outward * d for d in range(WIN, 0, -1)]
    near_last = [outward * -d for d in range(WIN, 0, -1)]

    middle = remote(
        wina.at[pl.ds(OWN, BLK_DEV)], winb.at[pl.ds(OWN, BLK_DEV)], cross_send, cross_recv, partner
    )
    start(middle)

    def over_there(distances):
        return halo(wina, winb, True, cross_send, cross_recv, distances)

    def over_here(distances):
        return halo(wina, wina, False, halo_send.at[0], halo_recv.at[0], distances)

    for_each(
        over_there([1, -1]) + over_here(far_first) + over_there([2, -2, 3, -3, 4, -4])
        + over_here(near_last),
        start,
    )
    start(swap)

    inverse = []
    for b in range(BLK_DEV):
        where_to = lax.broadcasted_iota(jnp.int32, (BLOCK, BLOCK), 0)
        onehot = jnp.where(
            jnp.broadcast_to(mirror_ref[b : b + 1, :], (BLOCK, BLOCK)) == where_to, 1.0, 0.0
        ).astype(jnp.bfloat16)
        lanes = lax.broadcasted_iota(jnp.int32, (16, BLOCK), 1).astype(jnp.float32).astype(jnp.bfloat16)
        found = lax.dot_general(
            lanes, onehot, (((1,), (1,)), ((), ())), preferred_element_type=jnp.float32
        )
        inverse.append(found[:NRHS].astype(jnp.int32))

    lane = lax.broadcasted_iota(jnp.int32, (NRHS, BLOCK), 1)
    sublane = lax.broadcasted_iota(jnp.int32, (NRHS, BLOCK), 0)
    sign = jnp.where(is_port, 1.0, -1.0)

    z = [[None] * BLK_DEV for _ in range(ITERS + 1)]
    for load in loads[2:]:
        load.wait()
    where_from = [
        jnp.clip(cols_ref[0, e] - (owner - WIN) * BLK_DEV, 0, SLOTS - 1) for e in range(NB_DEV)
    ]
    upper = [(rows_ref[0, e] == 0).astype(jnp.float32) for e in range(NB_DEV)]

    for e in range(NB_DEV):
        nb[e] = jnp.transpose(nb[e])

    def products(windows):
        total = jnp.zeros((16 * len(windows), BLOCK), jnp.float32)
        for e in range(0, NB_DEV, 2):
            lefts, rights = [], []
            for f in (e, e + 1):
                parts = []
                for window in windows:
                    picked = window[where_from[f]].astype(jnp.float32)
                    parts += [picked * upper[f], picked * (1.0 - upper[f])]
                lefts.append(jnp.concatenate(parts, axis=0).astype(jnp.bfloat16))
                rights.append(nb[f])
            total = total + lax.dot_general(
                jnp.concatenate(lefts, axis=1),
                jnp.concatenate(rights, axis=0),
                (((1,), (0,)), ((), ())),
                preferred_element_type=jnp.float32,
            )
        return total

    def with_pairs(partial, pairs):
        for i, j in pairs:
            product = z[i][0] * z[j][0] + z[i][1] * z[j][1]
            partial = jnp.where(
                lane == PAIRS.index((i, j)) * NRHS + sublane,
                jnp.sum(product, axis=1, keepdims=True),
                partial,
            )
        return partial

    for k in range(ITERS):
        if k > 0:
            window = (None, win1, win2)[k]
            for b in range(BLK_DEV):
                window[OWN + b] = z[k][b].astype(jnp.bfloat16)
            for_each(
                halo(window, window, False, halo_send.at[k], halo_recv.at[k], far_first + near_last),
                start,
            )
            for b in range(BLK_DEV):
                zs[k - 1, b] = z[k][b]
        if k == ITERS - 1:
            received(swap)
            for b in range(BLK_DEV):
                z[0][b] = xr[b] + sign * xs[b]
            partial = with_pairs(
                jnp.zeros((NRHS, BLOCK), jnp.float32), [p for p in PAIRS if p[1] < ITERS]
            )
        wait_near(wina if k == 0 else window, halo_recv.at[k])
        if k == 0:
            wait_near(winb, cross_recv, 1)
            total = products([wina, winb])
            total = sign * total[:16] + total[16:]
        else:
            total = products([window])
        z[k + 1] = [total[:NRHS], total[NRHS:]]

    partial = with_pairs(partial, [p for p in PAIRS if p[1] == ITERS])
    row = jnp.sum(partial, axis=0, keepdims=True)

    def total_of(red, size):
        parts = [red[n] for n in range(size)]
        while len(parts) > 1:
            parts = [a + b for a, b in zip(parts[::2], parts[1::2], strict=True)]
        return parts[0]

    red0[column] = row

    def to_column(flip):
        return remote(
            red0.at[column], red0.at[column], red_send.at[0], red_recv.at[0], in_column(flip, 0)
        )

    early_copies = [to_column(flip) for flip in range(8)]

    @pl.when(is_early)
    def _():
        for copy in early_copies[1:]:
            start(copy)

    @pl.when(jnp.logical_not(is_early))
    def _():
        for z_to in range(EARLY):
            for core_flip in range(2):
                start(to_column((grp % EARLY ^ z_to) * 2 + core_flip))

    for b in range(BLK_DEV):
        zs[ITERS - 1, b] = z[ITERS][b]
    exchange = remote(zs, zr, zx_send, zx_recv, partner)
    start(exchange)
    copies.append(exchange)

    def to_plane(flip):
        return remote(
            red1.at[spot], red1.at[spot], red_send.at[1], red_recv.at[1], in_plane(flip)
        )

    passes = grp == EARLY - 1
    pass_on = [
        remote(total_ref, total_ref, pass_send.at[n], pass_recv, (side, EARLY + n, dev))
        for n in range(N_GRP - EARLY)
    ]

    @pl.when(is_early)
    def _():
        wait_bytes(red0, STAGE_SIZES[0] - 1, red_recv.at[0])
        red1[spot] = total_of(red0, STAGE_SIZES[0])
        for y_to in (0, 1, 2, 3, 7, 4, 5, 6):
            y_flip = spot % 8 ^ y_to
            for x_flip in (2, 1, 3):
                start(to_plane(x_flip * 8 + y_flip))

            @pl.when(y_flip > 0)
            def _(y_flip=y_flip):
                start(to_plane(y_flip))


    received(exchange)
    images = [own]
    for k in range(ITERS):
        image = []
        for b in range(BLK_DEV):
            mine, other = z[k + 1][b], zr[k, b]
            port = 0.5 * (mine + other)
            starboard = lane_gather(0.5 * (other - mine), inverse[b])
            image.append(jnp.where(is_port, port, starboard))
        images.append(image)

    for copy in copies:
        sent_off(copy)
    wait_near(winb, cross_send, 1)
    for k, window in enumerate((wina, win1, win2)):
        wait_near(window, halo_send.at[k])

    @pl.when(is_early)
    def _():
        wait_bytes(red0, 7, red_send.at[0])

    @pl.when(jnp.logical_not(is_early))
    def _():
        wait_bytes(red0, 8, red_send.at[0])

    @pl.when(is_early)
    def _():
        wait_bytes(red1, STAGE_SIZES[1] - 1, red_recv.at[1])

    @pl.when(passes)
    def _():
        total_ref[...] = total_of(red1, STAGE_SIZES[1])
        for copy in pass_on:
            start(copy)

    @pl.when(jnp.logical_not(is_early))
    def _():
        received(pass_on[0])

    row = jnp.where(is_early, total_of(red1, STAGE_SIZES[1]), total_ref[...])
    spread = jnp.broadcast_to(row * (0.5 / TOTAL_PANELS), (NRHS, BLOCK))
    gram = {}
    for p, pair in enumerate(PAIRS):
        chosen = jnp.where(lane == p * NRHS + sublane, spread, 0.0)
        gram[pair] = jnp.broadcast_to(jnp.sum(chosen, axis=1, keepdims=True), (NRHS, BLOCK))
    c, h = coefficients(gram)
    for j in range(ITERS + 1):
        for b in range(BLK_DEV):
            value = c[j][0] * images[0][b]
            for i in range(1, j + 1):
                value = value + c[j][i] * images[i][b]
            q_ref[j, 0, :, b * BLOCK : (b + 1) * BLOCK] = value
    table = jnp.zeros((NRHS, BLOCK), jnp.float32)
    for (j, k), value in h.items():
        table = jnp.where(lane == k * (ITERS + 1) + j, value, table)
    turned = jnp.transpose(table)
    for k in range(ITERS):
        h_ref[k] = turned[k * (ITERS + 1) : (k + 1) * (ITERS + 1), :]

    @pl.when(is_early)
    def _():
        wait_bytes(red1, STAGE_SIZES[1] - 1, red_send.at[1])

    @pl.when(passes)
    def _():
        for copy in pass_on:
            sent_off(copy)


def settle(q_ref, h_ref, q_out, h_out, sem):
    moves = [
        pltpu.make_async_copy(q_ref, q_out, sem.at[0]),
        pltpu.make_async_copy(h_ref, h_out, sem.at[1]),
    ]
    for move in moves:
        move.start()
    for move in moves:
        move.wait()


def on_device(sources, near_blocks, block_rows, block_cols, mirror):
    vmem = pl.BlockSpec(memory_space=pltpu.VMEM)
    hbm = pl.BlockSpec(memory_space=pltpu.HBM)
    f32, bf16 = jnp.float32, jnp.bfloat16
    dma = pltpu.SemaphoreType.DMA
    window = pltpu.VMEM((SLOTS, NRHS, BLOCK), bf16)
    blocks = pltpu.VMEM((BLK_DEV, NRHS, BLOCK), f32)
    steps = pltpu.VMEM((ITERS, BLK_DEV, NRHS, BLOCK), f32)
    q, h = pl.pallas_call(
        kernel,
        out_shape=(
            jax.ShapeDtypeStruct((ITERS + 1, 1, NRHS, BLK_DEV * BLOCK), f32),
            jax.ShapeDtypeStruct((ITERS, ITERS + 1, NRHS), f32),
        ),
        in_specs=[hbm] * 5,
        out_specs=(vmem, vmem),
        scratch_shapes=[
            pltpu.VMEM((1, NRHS, BLK_DEV * BLOCK), f32),
            pltpu.VMEM((NB_DEV, BLOCK, BLOCK), bf16),
            pltpu.SMEM((1, NB_DEV), jnp.int32),
            pltpu.SMEM((1, NB_DEV), jnp.int32),
            pltpu.VMEM((BLK_DEV, BLOCK), jnp.int32),
            window, window, window, window,
            blocks, blocks,
            steps, steps,
            *[pltpu.VMEM((size, 1, BLOCK), f32) for size in STAGE_SIZES],
            pltpu.VMEM((1, BLOCK), f32),
            dma((5,)),
            dma, dma,
            dma, dma,
            dma((ITERS,)), dma((ITERS,)),
            dma, dma,
            dma((2,)), dma((2,)),
            dma((N_GRP - EARLY,)), dma,
        ],
        compiler_params=pltpu.CompilerParams(
            collective_id=0, has_side_effects=True, vmem_limit_bytes=8 * 1024 * 1024
        ),
    )(
        *[
            pltpu.with_memory_space_constraint(operand, pltpu.HBM)
            for operand in (
                sources, near_blocks, block_rows, block_cols, mirror.reshape(BLK_DEV, BLOCK)
            )
        ]
    )
    q, h = pl.pallas_call(
        settle,
        out_shape=(
            jax.ShapeDtypeStruct(q.shape, f32),
            jax.ShapeDtypeStruct(h.shape, f32),
        ),
        in_specs=[vmem, vmem],
        out_specs=(hbm, hbm),
        scratch_shapes=[dma((2,))],
        compiler_params=pltpu.CompilerParams(vmem_limit_bytes=8 * 1024 * 1024),
    )(q, h)
    return q, jnp.transpose(h)


def solution(mesh):
    placed = (
        P("side", None, ("grp", "dev")),
        P("side", ("grp", "dev"), None, None),
        P("side", ("grp", "dev")),
        P("side", ("grp", "dev")),
        P(("grp", "dev")),
    )
    return jax.shard_map(
        on_device,
        mesh=mesh,
        in_specs=placed,
        out_specs=(P(None, "side", None, ("grp", "dev")), P()),
        check_vma=False,
    )
```

```python
import jax
import jax.numpy as jnp
from jax import lax
from jax.experimental import pallas as pl
from jax.experimental.pallas import tpu as pltpu
from jax.sharding import PartitionSpec as P

BLOCK = 128
BLK_DEV = 2
WIN = 4
ITERS = 3
NB_DEV = 32
NRHS = 8
N_GRP = 8
N_DEV = 32
TOTAL_PANELS = 131072.0
EPSILON = 1e-06
SLOTS = (2 * WIN + 1) * BLK_DEV
OWN = WIN * BLK_DEV
MESH = pl.DeviceIdType.MESH
PAIRS = [(i, j) for j in range(ITERS + 1) for i in range(j + 1)]
N_OWNERS = N_GRP * N_DEV
STAGE_SIZES = (16, 32)
EARLY = N_GRP // 2
X_HOPS = (0, 1, 2, 1)
Y_HOPS = (0, 1, 2, 3, 4, 3, 2, 3)
FLIPS = sorted(range(1, 32), key=lambda f: -X_HOPS[f // 8] - Y_HOPS[f % 8])
DISTANCES = [4, -4, 3, -3, 2, -2, 1, -1]


def lane_gather(x, index):
    return jnp.take_along_axis(x, index, axis=1, mode="promise_in_bounds")


def coefficients(gram):
    def dot(a, b):
        total = None
        for i, ai in enumerate(a):
            row = None
            for j, bj in enumerate(b):
                term = gram[(min(i, j), max(i, j))] * bj
                row = term if row is None else row + term
            total = ai * row if total is None else total + ai * row
        return total

    c = [[1.0 / jnp.sqrt(gram[(0, 0)] + EPSILON)]]
    h = {}
    for k in range(ITERS):
        w = [0.5 * v for v in c[k]] + [c[k][k]]
        for i in range(1, k + 1):
            w[i] = w[i] + c[k][i - 1]
        u = list(w)
        for j in range(k + 1):
            h[(j, k)] = dot(w, c[j])
            for i in range(j + 1):
                u[i] = u[i] - h[(j, k)] * c[j][i]
        norm = jnp.sqrt(jnp.maximum(dot(u, u), 0.0) + EPSILON)
        h[(k + 1, k)] = norm
        inverse = 1.0 / norm
        c.append([v * inverse for v in u])
    return c, h


def kernel(
    x_hbm, nb_hbm, rows_hbm, cols_hbm, mirror_hbm, q_ref, h_ref,
    x_ref, nb, rows_ref, cols_ref, mirror_ref,
    wina, winb, win1, win2, xs, xr, zs, zr, red0, red1, total_ref, upper_mask,
    load_sem, swap_send, swap_recv, cross_send, cross_recv, halo_send, halo_recv,
    zx_send, zx_recv, red_send, red_recv, pass_send, pass_recv,
):
    side = lax.axis_index("side")
    grp = lax.axis_index("grp")
    dev = lax.axis_index("dev")
    owner = grp * N_DEV + dev
    is_port = side == 0
    chip_x, y_lo, core = dev // 8, (dev // 2) % 4, dev % 2
    is_early = grp < EARLY
    is_edge = (owner < WIN) | (owner >= N_OWNERS - WIN)
    column = grp * 2 + core
    spot = chip_x * 8 + side * 4 + y_lo

    def exists(distance):
        return (owner + distance >= 0) & (owner + distance < N_OWNERS)

    partner = (1 - side, grp, dev)

    def near(distance, across):
        other = owner + distance
        return (1 - side if across else side, other // N_DEV, other % N_DEV)

    def in_column(flip, half):
        return (side, half + (grp % EARLY ^ (flip // 2)), chip_x * 8 + y_lo * 2 + (core ^ (flip % 2)))

    def in_plane(flip):
        other = spot ^ flip
        return ((other // 4) % 2, grp, (other // 8) * 8 + (other % 4) * 2 + core)

    def for_each(items, act):
        @pl.when(jnp.logical_not(is_edge))
        def _():
            for _, item in items:
                act(item)

        @pl.when(is_edge)
        def _():
            for d, item in items:

                @pl.when(exists(d))
                def _(item=item):
                    act(item)

    n_near = 0
    for d in DISTANCES:
        n_near = n_near + exists(d).astype(jnp.int32)

    def wait_bytes(ref, count, sem):
        part = ref.at[pl.ds(0, count)]
        pltpu.make_async_copy(part, part, sem).wait()

    def wait_near(ref, sem, extra=0):
        @pl.when(jnp.logical_not(is_edge))
        def _():
            wait_bytes(ref, (2 * WIN + extra) * BLK_DEV, sem)

        @pl.when(is_edge)
        def _():
            for m in range(WIN, 2 * WIN):

                @pl.when(n_near == m)
                def _(m=m):
                    wait_bytes(ref, (m + extra) * BLK_DEV, sem)

    loads = [
        pltpu.make_async_copy(source, target, load_sem.at[n])
        for n, (source, target) in enumerate(
            (
                (x_hbm, x_ref),
                (mirror_hbm, mirror_ref),
                (cols_hbm, cols_ref),
                (rows_hbm, rows_ref),
                (nb_hbm.at[0], nb),
            )
        )
    ]
    for load in loads:
        load.start()

    barrier = pltpu.get_barrier_semaphore()

    def greet(device):
        pl.semaphore_signal(barrier, inc=1, device_id=device, device_id_type=MESH)

    neighbours = [(d, near(d, across)) for d in DISTANCES for across in (False, True)]
    greet(partner)
    for_each(neighbours, greet)

    @pl.when(is_early)
    def _():
        for flip in FLIPS:
            greet(in_plane(flip))
        for flip in range(1, 8):
            greet(in_column(flip, 0))
        for flip in range(8):
            greet(in_column(flip, EARLY))

    loads[0].wait()
    loads[1].wait()

    index = [
        jnp.broadcast_to(mirror_ref[b : b + 1, :], (NRHS, BLOCK)) for b in range(BLK_DEV)
    ]
    own = [x_ref[0, :, b * BLOCK : (b + 1) * BLOCK] for b in range(BLK_DEV)]
    star = [lane_gather(own[b], index[b]) for b in range(BLK_DEV)]
    for b in range(BLK_DEV):
        sent = jnp.where(is_port, own[b], star[b])
        xs[b] = sent
        wina[OWN + b] = sent.astype(jnp.bfloat16)

    pl.semaphore_wait(barrier, 1 + 2 * n_near + jnp.where(is_early, len(FLIPS) + 7, 8))

    def remote(source, target, send_sem, recv_sem, device):
        return pltpu.make_async_remote_copy(
            src_ref=source, dst_ref=target, send_sem=send_sem, recv_sem=recv_sem,
            device_id=device, device_id_type=MESH,
        )

    def start(copy):
        copy.start()

    def received(copy):
        copy.wait_recv()

    def sent_off(copy):
        copy.wait_send()

    swap = remote(xs, xr, swap_send, swap_recv, partner)
    copies = [swap]

    def halo(window, target, across, send_sem, recv_sem, distances):
        return [
            (
                d,
                remote(
                    window.at[pl.ds(OWN, BLK_DEV)],
                    target.at[pl.ds((WIN - d) * BLK_DEV, BLK_DEV)],
                    send_sem, recv_sem, near(d, across),
                ),
            )
            for d in distances
        ]

    outward = jnp.where(y_lo >= 2, 1, -1)
    far_first = [outward * d for d in range(WIN, 0, -1)]
    near_last = [outward * -d for d in range(WIN, 0, -1)]

    middle = remote(
        wina.at[pl.ds(OWN, BLK_DEV)], winb.at[pl.ds(OWN, BLK_DEV)], cross_send, cross_recv, partner
    )
    start(middle)

    def over_there(distances):
        return halo(wina, winb, True, cross_send, cross_recv, distances)

    def over_here(distances):
        return halo(wina, wina, False, halo_send.at[0], halo_recv.at[0], distances)

    for_each(
        over_there([1, -1]) + over_here(far_first) + over_there([2, -2, 3, -3, 4, -4])
        + over_here(near_last),
        start,
    )
    start(swap)

    inverse = []
    for b in range(BLK_DEV):
        where_to = lax.broadcasted_iota(jnp.int32, (BLOCK, BLOCK), 0)
        onehot = jnp.where(
            jnp.broadcast_to(mirror_ref[b : b + 1, :], (BLOCK, BLOCK)) == where_to, 1.0, 0.0
        ).astype(jnp.bfloat16)
        lanes = lax.broadcasted_iota(jnp.int32, (16, BLOCK), 1).astype(jnp.float32).astype(jnp.bfloat16)
        found = lax.dot_general(
            lanes, onehot, (((1,), (1,)), ((), ())), preferred_element_type=jnp.float32
        )
        inverse.append(found[:NRHS].astype(jnp.int32))

    lane = lax.broadcasted_iota(jnp.int32, (NRHS, BLOCK), 1)
    sublane = lax.broadcasted_iota(jnp.int32, (NRHS, BLOCK), 0)
    sign = jnp.where(is_port, 1.0, -1.0)

    z = [[None] * BLK_DEV for _ in range(ITERS + 1)]
    for load in loads[2:]:
        load.wait()
    where_from = [
        jnp.clip(cols_ref[0, e] - (owner - WIN) * BLK_DEV, 0, SLOTS - 1) for e in range(NB_DEV)
    ]
    upper = [(rows_ref[0, e] == 0).astype(jnp.float32) for e in range(NB_DEV)]

    for e in range(NB_DEV):
        nb[e] = jnp.transpose(nb[e])

    for e in range(NB_DEV):
        upper_mask[e] = jnp.full((NRHS, BLOCK), upper[e], jnp.float32)

    def products(windows):
        total = jnp.zeros((16 * len(windows), BLOCK), jnp.float32)
        for e in range(0, NB_DEV, 2):
            lefts, rights = [], []
            for f in (e, e + 1):
                parts = []
                for window in windows:
                    picked = window[where_from[f]].astype(jnp.float32)
                    first = picked * upper_mask[f]
                    parts += [first, picked - first]
                lefts.append(jnp.concatenate(parts, axis=0).astype(jnp.bfloat16))
                rights.append(nb[f])
            total = total + lax.dot_general(
                jnp.concatenate(lefts, axis=1),
                jnp.concatenate(rights, axis=0),
                (((1,), (0,)), ((), ())),
                preferred_element_type=jnp.float32,
            )
        return total

    def with_pairs(partial, pairs):
        for i, j in pairs:
            product = z[i][0] * z[j][0] + z[i][1] * z[j][1]
            partial = jnp.where(
                lane == PAIRS.index((i, j)) * NRHS + sublane,
                jnp.sum(product, axis=1, keepdims=True),
                partial,
            )
        return partial

    for k in range(ITERS):
        if k > 0:
            window = (None, win1, win2)[k]
            for b in range(BLK_DEV):
                window[OWN + b] = z[k][b].astype(jnp.bfloat16)
            for_each(
                halo(window, window, False, halo_send.at[k], halo_recv.at[k], far_first + near_last),
                start,
            )
            for b in range(BLK_DEV):
                zs[k - 1, b] = z[k][b]
        if k == ITERS - 1:
            received(swap)
            for b in range(BLK_DEV):
                z[0][b] = xr[b] + sign * xs[b]
            partial = with_pairs(
                jnp.zeros((NRHS, BLOCK), jnp.float32), [p for p in PAIRS if p[1] < ITERS]
            )
        wait_near(wina if k == 0 else window, halo_recv.at[k])
        if k == 0:
            wait_near(winb, cross_recv, 1)
            total = products([wina, winb])
            total = sign * total[:16] + total[16:]
        else:
            total = products([window])
        z[k + 1] = [total[:NRHS], total[NRHS:]]

    partial = with_pairs(partial, [p for p in PAIRS if p[1] == ITERS])
    row = jnp.sum(partial, axis=0, keepdims=True)

    def total_of(red, size):
        parts = [red[n] for n in range(size)]
        while len(parts) > 1:
            parts = [a + b for a, b in zip(parts[::2], parts[1::2], strict=True)]
        return parts[0]

    red0[column] = row

    def to_column(flip):
        return remote(
            red0.at[column], red0.at[column], red_send.at[0], red_recv.at[0], in_column(flip, 0)
        )

    early_copies = [to_column(flip) for flip in range(8)]

    @pl.when(is_early)
    def _():
        for copy in early_copies[1:]:
            start(copy)

    @pl.when(jnp.logical_not(is_early))
    def _():
        for z_to in range(EARLY):
            for core_flip in range(2):
                start(to_column((grp % EARLY ^ z_to) * 2 + core_flip))

    for b in range(BLK_DEV):
        zs[ITERS - 1, b] = z[ITERS][b]
    exchange = remote(zs, zr, zx_send, zx_recv, partner)
    start(exchange)
    copies.append(exchange)

    def to_plane(flip):
        return remote(
            red1.at[spot], red1.at[spot], red_send.at[1], red_recv.at[1], in_plane(flip)
        )

    passes = grp == EARLY - 1
    pass_on = [
        remote(total_ref, total_ref, pass_send.at[n], pass_recv, (side, EARLY + n, dev))
        for n in range(N_GRP - EARLY)
    ]

    @pl.when(is_early)
    def _():
        wait_bytes(red0, STAGE_SIZES[0] - 1, red_recv.at[0])
        red1[spot] = total_of(red0, STAGE_SIZES[0])
        for y_to in (0, 1, 2, 3, 7, 4, 5, 6):
            y_flip = spot % 8 ^ y_to
            for x_flip in (2, 1, 3):
                start(to_plane(x_flip * 8 + y_flip))

            @pl.when(y_flip > 0)
            def _(y_flip=y_flip):
                start(to_plane(y_flip))


    received(exchange)
    images = [own]
    for k in range(ITERS):
        image = []
        for b in range(BLK_DEV):
            mine, other = z[k + 1][b], zr[k, b]
            port = 0.5 * (mine + other)
            starboard = lane_gather(0.5 * (other - mine), inverse[b])
            image.append(jnp.where(is_port, port, starboard))
        images.append(image)

    for copy in copies:
        sent_off(copy)
    wait_near(winb, cross_send, 1)
    for k, window in enumerate((wina, win1, win2)):
        wait_near(window, halo_send.at[k])

    @pl.when(is_early)
    def _():
        wait_bytes(red0, 7, red_send.at[0])

    @pl.when(jnp.logical_not(is_early))
    def _():
        wait_bytes(red0, 8, red_send.at[0])

    @pl.when(is_early)
    def _():
        wait_bytes(red1, STAGE_SIZES[1] - 1, red_recv.at[1])

    @pl.when(passes)
    def _():
        total_ref[...] = total_of(red1, STAGE_SIZES[1])
        for copy in pass_on:
            start(copy)

    @pl.when(jnp.logical_not(is_early))
    def _():
        received(pass_on[0])

    row = jnp.where(is_early, total_of(red1, STAGE_SIZES[1]), total_ref[...])
    spread = jnp.broadcast_to(row * (0.5 / TOTAL_PANELS), (NRHS, BLOCK))
    gram = {}
    for p, pair in enumerate(PAIRS):
        chosen = jnp.where(lane == p * NRHS + sublane, spread, 0.0)
        gram[pair] = jnp.broadcast_to(jnp.sum(chosen, axis=1, keepdims=True), (NRHS, BLOCK))
    c, h = coefficients(gram)
    for j in range(ITERS + 1):
        for b in range(BLK_DEV):
            value = c[j][0] * images[0][b]
            for i in range(1, j + 1):
                value = value + c[j][i] * images[i][b]
            q_ref[j, 0, :, b * BLOCK : (b + 1) * BLOCK] = value
    table = jnp.zeros((NRHS, BLOCK), jnp.float32)
    for (j, k), value in h.items():
        table = jnp.where(lane == k * (ITERS + 1) + j, value, table)
    turned = jnp.transpose(table)
    for k in range(ITERS):
        h_ref[k] = turned[k * (ITERS + 1) : (k + 1) * (ITERS + 1), :]

    @pl.when(is_early)
    def _():
        wait_bytes(red1, STAGE_SIZES[1] - 1, red_send.at[1])

    @pl.when(passes)
    def _():
        for copy in pass_on:
            sent_off(copy)


def settle(q_ref, h_ref, q_out, h_out, sem):
    moves = [
        pltpu.make_async_copy(q_ref, q_out, sem.at[0]),
        pltpu.make_async_copy(h_ref, h_out, sem.at[1]),
    ]
    for move in moves:
        move.start()
    for move in moves:
        move.wait()


def on_device(sources, near_blocks, block_rows, block_cols, mirror):
    vmem = pl.BlockSpec(memory_space=pltpu.VMEM)
    hbm = pl.BlockSpec(memory_space=pltpu.HBM)
    f32, bf16 = jnp.float32, jnp.bfloat16
    dma = pltpu.SemaphoreType.DMA
    window = pltpu.VMEM((SLOTS, NRHS, BLOCK), bf16)
    blocks = pltpu.VMEM((BLK_DEV, NRHS, BLOCK), f32)
    steps = pltpu.VMEM((ITERS, BLK_DEV, NRHS, BLOCK), f32)
    q, h = pl.pallas_call(
        kernel,
        out_shape=(
            jax.ShapeDtypeStruct((ITERS + 1, 1, NRHS, BLK_DEV * BLOCK), f32),
            jax.ShapeDtypeStruct((ITERS, ITERS + 1, NRHS), f32),
        ),
        in_specs=[hbm] * 5,
        out_specs=(vmem, vmem),
        scratch_shapes=[
            pltpu.VMEM((1, NRHS, BLK_DEV * BLOCK), f32),
            pltpu.VMEM((NB_DEV, BLOCK, BLOCK), bf16),
            pltpu.SMEM((1, NB_DEV), jnp.int32),
            pltpu.SMEM((1, NB_DEV), jnp.int32),
            pltpu.VMEM((BLK_DEV, BLOCK), jnp.int32),
            window, window, window, window,
            blocks, blocks,
            steps, steps,
            *[pltpu.VMEM((size, 1, BLOCK), f32) for size in STAGE_SIZES],
            pltpu.VMEM((1, BLOCK), f32),
            pltpu.VMEM((NB_DEV, NRHS, BLOCK), f32),
            dma((5,)),
            dma, dma,
            dma, dma,
            dma((ITERS,)), dma((ITERS,)),
            dma, dma,
            dma((2,)), dma((2,)),
            dma((N_GRP - EARLY,)), dma,
        ],
        compiler_params=pltpu.CompilerParams(
            collective_id=0, has_side_effects=True, vmem_limit_bytes=8 * 1024 * 1024
        ),
    )(
        *[
            pltpu.with_memory_space_constraint(operand, pltpu.HBM)
            for operand in (
                sources, near_blocks, block_rows, block_cols, mirror.reshape(BLK_DEV, BLOCK)
            )
        ]
    )
    q, h = pl.pallas_call(
        settle,
        out_shape=(
            jax.ShapeDtypeStruct(q.shape, f32),
            jax.ShapeDtypeStruct(h.shape, f32),
        ),
        in_specs=[vmem, vmem],
        out_specs=(hbm, hbm),
        scratch_shapes=[dma((2,))],
        compiler_params=pltpu.CompilerParams(vmem_limit_bytes=8 * 1024 * 1024),
    )(q, h)
    return q, jnp.transpose(h)


def solution(mesh):
    placed = (
        P("side", None, ("grp", "dev")),
        P("side", ("grp", "dev"), None, None),
        P("side", ("grp", "dev")),
        P("side", ("grp", "dev")),
        P(("grp", "dev")),
    )
    return jax.shard_map(
        on_device,
        mesh=mesh,
        in_specs=placed,
        out_specs=(P(None, "side", None, ("grp", "dev")), P()),
        check_vma=False,
    )
```
